32 devices in a mesh: dp: 8 (over z, y), tensor: 4 (over x, core).
Axes of the slice: x: 2, y: 2, z: 4, core: 2. Of those that a mesh axis runs over, the one named last changes fastest.
Arguments:
- tokens: bfloat16 [2048, 768], P('dp'), may hold values from -6 to 6
- cotangent: bfloat16 [2048, 768], P('dp'), may hold values from -6 to 6
- norm_gain: float32 [2, 768], replicated, may hold values from 0.5 to 1.5
- w_z: bfloat16 [2, 768, 1536], P(None, None, 'tensor'), may hold values from -0.21875 to 0.21875
- w_x: bfloat16 [2, 768, 1536], P(None, None, 'tensor'), may hold values from -0.21875 to 0.21875
- w_bc: bfloat16 [2, 768, 256], replicated, may hold values from -0.21875 to 0.21875
- w_dt: bfloat16 [2, 768, 24], P(None, None, 'tensor'), may hold values from -0.21875 to 0.21875
- conv_x: float32 [2, 4, 1536], P(None, None, 'tensor'), may hold values from -3 to 3
- conv_x_bias: float32 [2, 1536], P(None, 'tensor'), may hold values from -3 to 3
- conv_bc: float32 [2, 4, 256], replicated, may hold values from -3 to 3
- conv_bc_bias: float32 [2, 256], replicated, may hold values from -3 to 3
- dt_bias: float32 [2, 24], P(None, 'tensor'), may hold values from -6 to -2
- a_log: float32 [2, 24], P(None, 'tensor'), may hold values from 0 to 2.77
- d_skip: float32 [2, 24], P(None, 'tensor'), may hold values from 0.5 to 1.5
- gate_gain: float32 [2, 1536], P(None, 'tensor'), may hold values from 0.5 to 1.5
- w_out: bfloat16 [2, 1536, 768], P(None, 'tensor'), may hold values from -0.15625 to 0.15625
Outputs:
- output: float32 [2048, 768], P('dp')
- input_grad: float32 [2048, 768], P('dp')
- grad_norm_gain: float32 [2, 768], P(None, 'dp')
- grad_w_z: float32 [2, 768, 1536], P(None, 'dp', 'tensor')
- grad_w_x: float32 [2, 768, 1536], P(None, 'dp', 'tensor')
- grad_w_dt: float32 [2, 768, 24], P(None, 'dp', 'tensor')
- grad_w_out: float32 [2, 1536, 768], P(None, 'tensor', 'dp')
- grad_channels: float32 [2, 6, 24, 64], P(None, None, 'tensor', 'dp')
- grad_w_bc: float32 [2, 768, 256], P(None, ('dp', 'tensor'))
- grad_bc_conv: float32 [2, 5, 256], P(None, None, ('dp', 'tensor'))
- grad_heads: float32 [2, 3, 24], P(None, None, 'tensor')
The draws below stay inside these ranges and needn't reach their ends.
All inputs are finite; a program needn't handle non-finite values.
Results may differ from the reference program's by a relative error of at most 0.012.
Values sent between devices are 32-bit elements; how exact they have to be, the bound alone decides.
A program may use at most 128 MiB of HBM per device.

```python
import jax
import jax.numpy as jnp
from jax import lax

D = 768
INNER = 1536
HEADS = 24
P_SIZE = 64
N = 128
K = 4
GROUP = 128
LENGTH = 256
LAYERS = 2
SEQS = 8
TOKENS = 2048


def with_spikes(array, rng, source, target, blocks, factor):
    def block_of(position):
        return (jnp.arange(array.shape[position]) // (array.shape[position] // blocks)).reshape((-1,) + (1,) * (array.ndim - 1 - position))

    one_side = jax.random.permutation(rng, blocks)[block_of(target)]
    far = (block_of(target) + blocks // 2) % blocks
    return jnp.where((block_of(source) == one_side) | (block_of(source) == far), factor * array, array)


def level_of(stream_key, shape, cuts, least, high):
    level = 1.0
    for axis_at, parts in cuts:
        draws = jax.random.uniform(jax.random.fold_in(jax.random.fold_in(stream_key, 6), axis_at), (parts,), jnp.float32, least / len(cuts), high / len(cuts))
        level = level * jnp.repeat(jnp.exp(draws), shape[axis_at] // parts).reshape((-1,) + (1,) * (len(shape) - 1 - axis_at))
    return level


def noise(rng, dims, scale, most, shards=(), held_as=jnp.bfloat16):
    array = scale * jax.random.normal(rng, dims, jnp.float32)
    if shards:
        array = array * level_of(rng, dims, shards, -0.22, 0.18)
    return jnp.clip(array, -most, most).astype(held_as)


def noise_with(own_key, shape, scale, reach, pieces, heavy, kind=jnp.bfloat16):
    values = scale * jax.random.normal(own_key, shape, jnp.float32)
    if pieces:
        values = values * level_of(own_key, shape, pieces, -0.22, 0.18)
    return jnp.clip(with_spikes(values, jax.random.fold_in(own_key, 3), *heavy), -reach, reach).astype(kind)


def setup_inputs(seed: int = 0) -> dict:
    key_list = jax.random.split(jax.random.key(seed), 17)
    return {
        "tokens": noise_with(key_list[0], (TOKENS, D), 1.0, 6.0, ((0, 8),), (0, 1, 8, 2.0)),
        "cotangent": noise_with(key_list[1], (TOKENS, D), 1.0, 6.0, ((0, 8),), (0, 1, 8, 2.0)),
        "norm_gain": jnp.clip(1.0 + 0.1 * jax.random.normal(key_list[2], (LAYERS, D), jnp.float32), 0.5, 1.5),
        "w_z": noise(key_list[3], (LAYERS, D, INNER), D ** -0.5, 0.21875, ((2, 4),)),
        "w_x": noise(key_list[4], (LAYERS, D, INNER), D ** -0.5, 0.21875, ((2, 4),)),
        "w_bc": noise(key_list[5], (LAYERS, D, 2 * N), D ** -0.5, 0.21875),
        "w_dt": noise(key_list[6], (LAYERS, D, HEADS), D ** -0.5, 0.21875, ((2, 4),)),
        "conv_x": noise(key_list[7], (LAYERS, K, INNER), K ** -0.5, 3.0, ((2, 4),), jnp.float32),
        "conv_x_bias": noise(key_list[8], (LAYERS, INNER), 0.5, 3.0, ((1, 4),), jnp.float32),
        "conv_bc": noise(key_list[9], (LAYERS, K, 2 * N), K ** -0.5, 3.0, (), jnp.float32),
        "conv_bc_bias": noise(key_list[10], (LAYERS, 2 * N), 0.5, 3.0, (), jnp.float32),
        "dt_bias": jnp.clip(-6.0 + 4.0 * jax.random.uniform(key_list[11], (LAYERS, HEADS), jnp.float32) ** level_of(key_list[11], (LAYERS, HEADS), ((1, 4),), -0.2, 0.2), -6.0, -2.0),
        "a_log": jnp.clip(2.77 * jax.random.uniform(key_list[12], (LAYERS, HEADS), jnp.float32) ** level_of(key_list[12], (LAYERS, HEADS), ((1, 4),), -0.2, 0.2), 0.0, 2.77),
        "d_skip": jnp.clip(0.5 + 1.0 * jax.random.uniform(key_list[13], (LAYERS, HEADS), jnp.float32) ** level_of(key_list[13], (LAYERS, HEADS), ((1, 4),), -0.2, 0.2), 0.5, 1.5),
        "gate_gain": jnp.clip(1.0 + 0.1 * jax.random.normal(key_list[14], (LAYERS, INNER), jnp.float32), 0.5, 1.5),
        "w_out": noise(key_list[15], (LAYERS, INNER, D), INNER ** -0.5, 0.15625, ((1, 4),)),
    }


EPSILON = 1e-05
HIGHEST_PREC = lax.Precision.HIGHEST

def project(left, right):
    return jnp.dot(left, right, preferred_element_type=jnp.float32)

def causal_conv(signal, kernel, offset_vec):
    tap_count = kernel.shape[0]
    row_count = signal.shape[0]
    padded = jnp.pad(signal, ((tap_count - 1, 0), (0, 0)))
    running = jnp.zeros_like(signal) + offset_vec[None, :]
    for tap_index in range(tap_count):
        running = running + kernel[tap_index][None, :] * padded[tap_index:tap_index + row_count]
    return running

def mixer_core(inner_in, state_in, step_in, gate_in, kernel_x, shift_x, kernel_bc, shift_bc, step_bias, decay_log, skip_coef):
    length = inner_in.shape[0]
    head_count = step_in.shape[1]
    head_width = inner_in.shape[1] // head_count
    state_size = state_in.shape[1] // 2
    blocks = length // GROUP
    inner_conv = jax.nn.silu(causal_conv(inner_in, kernel_x, shift_x))
    state_conv = jax.nn.silu(causal_conv(state_in, kernel_bc, shift_bc))
    key_cols = state_conv[:, :state_size].reshape(blocks, GROUP, state_size)
    query_cols = state_conv[:, state_size:].reshape(blocks, GROUP, state_size)
    step_size = jax.nn.softplus(step_in + step_bias[None, :])
    log_rate = (step_size * (-jnp.exp(decay_log))[None, :]).reshape(blocks, GROUP, head_count)
    step_size = step_size.reshape(blocks, GROUP, head_count)
    values = inner_conv.reshape(blocks, GROUP, head_count, head_width)
    log_decay = jnp.cumsum(log_rate, axis=1)
    causal = jnp.tril(jnp.ones((GROUP, GROUP), dtype=bool))[None, :, :, None]
    log_gap = log_decay[:, :, None, :] - log_decay[:, None, :, :]
    decay_mask = jnp.where(causal, jnp.exp(jnp.where(causal, log_gap, 0.0)), 0.0)
    scores = jnp.einsum('qin,qjn->qij', query_cols, key_cols, precision=HIGHEST_PREC)
    weighted = values * step_size[..., None]
    block_weights = scores[..., None] * decay_mask
    within = jnp.einsum('qijh,qjhp->qihp', block_weights, weighted, precision=HIGHEST_PREC)
    to_end = jnp.exp(log_decay[:, -1:, :] - log_decay)
    states = jnp.einsum('qjn,qjhp->qhnp', key_cols, weighted * to_end[..., None], precision=HIGHEST_PREC)
    block_decay = jnp.exp(log_decay[:, -1, :])

    def carry_block(carried, inputs_pair):
        block_state, block_factor = inputs_pair
        return (carried * block_factor[:, None, None] + block_state, carried)
    initial = jnp.zeros((head_count, state_size, head_width), inner_in.dtype)
    _, before = lax.scan(carry_block, initial, (states, block_decay))
    across = jnp.einsum('qin,qhnp->qihp', query_cols, before, precision=HIGHEST_PREC) * jnp.exp(log_decay)[..., None]
    mixed = within + across + values * skip_coef[None, None, :, None]
    return mixed.reshape(length, head_count * head_width) * jax.nn.silu(gate_in)

def layer_forward(residual, params):
    norm_vec, wz_mat, wx_mat, wbc_mat, wdt_mat, kernel_x, shift_x, kernel_bc, shift_bc, step_bias, decay_log, skip_coef, gate_vec, wout_mat = params
    rescale = lax.rsqrt(lax.optimization_barrier(jnp.mean(residual * residual, axis=1, keepdims=True)) + EPSILON)
    normed = (residual * rescale * norm_vec[None, :]).astype(jnp.bfloat16)
    core_out = mixer_core(project(normed, wx_mat), project(normed, wbc_mat), project(normed, wdt_mat), project(normed, wz_mat), kernel_x, shift_x, kernel_bc, shift_bc, step_bias, decay_log, skip_coef)
    square = lax.optimization_barrier(jnp.mean(core_out * core_out, axis=1, keepdims=True))
    gated_out = (core_out * gate_vec[None, :]).astype(jnp.bfloat16)
    branch = project(gated_out, wout_mat)
    return residual + lax.rsqrt(square + EPSILON) * branch

def layer_backward(residual, params, upstream):
    norm_vec, wz_mat, wx_mat, wbc_mat, wdt_mat, kernel_x, shift_x, kernel_bc, shift_bc, step_bias, decay_log, skip_coef, gate_vec, wout_mat = params
    rescale = lax.rsqrt(lax.optimization_barrier(jnp.mean(residual * residual, axis=1, keepdims=True)) + EPSILON)
    normed = (residual * rescale * norm_vec[None, :]).astype(jnp.bfloat16)
    core_out, pull = jax.vjp(mixer_core, project(normed, wx_mat), project(normed, wbc_mat), project(normed, wdt_mat), project(normed, wz_mat), kernel_x, shift_x, kernel_bc, shift_bc, step_bias, decay_log, skip_coef)
    square = lax.optimization_barrier(jnp.mean(core_out * core_out, axis=1, keepdims=True))
    factor = lax.rsqrt(square + EPSILON)
    gated_out = (core_out * gate_vec[None, :]).astype(jnp.bfloat16)
    branch = project(gated_out, wout_mat)
    back_branch = (upstream * factor).astype(jnp.bfloat16)
    grad_wout = project(gated_out.T, back_branch)
    back_factor = lax.optimization_barrier(jnp.sum(upstream * branch, axis=1, keepdims=True))
    back_square = -0.5 * back_factor * factor * factor * factor
    back_gated = project(back_branch, wout_mat.T)
    grad_gate = lax.optimization_barrier(jnp.sum(back_gated * core_out, axis=0))
    back_core = back_gated * gate_vec[None, :] + back_square * 2.0 * core_out / INNER
    back_inner, back_state, back_step, back_gate, grad_kx, grad_sx, grad_kbc, grad_sbc, grad_bias, grad_decay, grad_skip = pull(back_core)
    back_inner = back_inner.astype(jnp.bfloat16)
    back_state = back_state.astype(jnp.bfloat16)
    back_step = back_step.astype(jnp.bfloat16)
    back_gate = back_gate.astype(jnp.bfloat16)
    grad_wz = project(normed.T, back_gate)
    grad_wx = project(normed.T, back_inner)
    grad_wbc = project(normed.T, back_state)
    grad_wdt = project(normed.T, back_step)
    back_normed = project(back_gate, wz_mat.T) + project(back_inner, wx_mat.T) + project(back_state, wbc_mat.T) + project(back_step, wdt_mat.T)
    grad_norm = lax.optimization_barrier(jnp.sum(back_normed * residual * rescale, axis=0))
    back_hat = back_normed * norm_vec[None, :]
    back_resid = upstream + rescale * back_hat - rescale * rescale * rescale * residual * lax.optimization_barrier(jnp.mean(back_hat * residual, axis=1, keepdims=True))
    grad_chan = jnp.concatenate([grad_kx, grad_sx[None, :], grad_gate[None, :]], axis=0)
    grad_bcconv = jnp.concatenate([grad_kbc, grad_sbc[None, :]], axis=0)
    grad_heads = jnp.stack([grad_decay, grad_skip, grad_bias])
    return (back_resid, (grad_norm, grad_wz, grad_wx, grad_wdt, grad_wout, grad_chan, grad_wbc, grad_bcconv, grad_heads))

def reference(tokens, cotangent, norm_gain, w_z, w_x, w_bc, w_dt, conv_x, conv_x_bias, conv_bc, conv_bc_bias, dt_bias, a_log, d_skip, gate_gain, w_out):
    all_params = (norm_gain, w_z, w_x, w_bc, w_dt, conv_x, conv_x_bias, conv_bc, conv_bc_bias, dt_bias, a_log, d_skip, gate_gain, w_out)

    def take_layer(layer_index):
        return tuple((param[layer_index] for param in all_params))
    zero_grads = (jnp.zeros((LAYERS, D), jnp.float32), jnp.zeros((LAYERS, D, INNER), jnp.float32), jnp.zeros((LAYERS, D, INNER), jnp.float32), jnp.zeros((LAYERS, D, HEADS), jnp.float32), jnp.zeros((LAYERS, INNER, D), jnp.float32), jnp.zeros((LAYERS, K + 2, INNER), jnp.float32), jnp.zeros((LAYERS, D, 2 * N), jnp.float32), jnp.zeros((LAYERS, K + 1, 2 * N), jnp.float32), jnp.zeros((LAYERS, 3, HEADS), jnp.float32))

    def one_sequence(totals, inputs_pair):
        seq_tokens, seq_cot = inputs_pair
        residual = seq_tokens.astype(jnp.float32)
        layer_inputs = []
        for layer_index in range(LAYERS):
            layer_inputs.append(residual)
            residual = layer_forward(residual, take_layer(layer_index))
        upstream = seq_cot.astype(jnp.float32)
        per_layer = [None] * LAYERS
        for layer_index in reversed(range(LAYERS)):
            upstream, per_layer[layer_index] = layer_backward(layer_inputs[layer_index], take_layer(layer_index), upstream)
        stacked = tuple((jnp.stack([per_layer[which][item] for which in range(LAYERS)]) for item in range(9)))
        totals = tuple((running + extra for running, extra in zip(totals, stacked)))
        return (totals, (residual, upstream))
    totals, (outputs, grads_in) = lax.scan(one_sequence, zero_grads, (tokens.reshape(SEQS, LENGTH, D), cotangent.reshape(SEQS, LENGTH, D)))
    return (outputs.reshape(TOKENS, D), grads_in.reshape(TOKENS, D), totals[0], totals[1], totals[2], totals[3], totals[4], totals[5].reshape(LAYERS, K + 2, HEADS, P_SIZE), totals[6], totals[7], totals[8])
```

```python
import functools
from types import SimpleNamespace
from typing import Any, NamedTuple

import jax
import jax.numpy as jnp
from jax import lax
from jax.experimental import pallas as pl
from jax.experimental.pallas import tpu as pltpu
from jax.sharding import PartitionSpec as P

P_SIZE = 64
K = 4
LANES = 128
DP, TENSOR = "dp", "tensor"
LENGTH = 256
LAYERS = 2
EPSILON = 1e-05
HIGHEST_PREC = lax.Precision.HIGHEST
MESH = pl.DeviceIdType.MESH
ROWS_ROWS = ((0,), (0,))
COLS_COLS = ((1,), (1,))


def matmul(left, right, dims=((1,), (0,)), precision=None):
    return lax.dot_general(
        left, right, (dims, ((), ())), precision=precision, preferred_element_type=jnp.float32
    )


def exact(left, right, dims=((1,), (0,))):
    return matmul(left, right, dims, HIGHEST_PREC)


def sigmoid(value):
    return 1.0 / (1.0 + jnp.exp(-value))


def softplus(value):
    return jnp.maximum(value, 0.0) + jnp.log1p(jnp.exp(-jnp.abs(value)))


def delayed(signal, shift):
    if shift == 0:
        return signal
    rows = signal.shape[0]
    moved = pltpu.roll(signal, shift % rows, 0)
    at = lax.broadcasted_iota(jnp.int32, signal.shape, 0)
    inside = at >= shift if shift > 0 else at < rows + shift
    return jnp.where(inside, moved, 0.0)


def causal_conv(signal, taps, offset):
    total = offset
    for k in range(K):
        total = total + taps[k : k + 1, :] * delayed(signal, K - 1 - k)
    return total


def conv_back(signal, taps, back):
    total = jnp.zeros_like(signal)
    tap_grads = []
    for k in range(K):
        total = total + taps[k : k + 1, :] * delayed(back, k + 1 - K)
        tap_grads.append(jnp.sum(back * delayed(signal, K - 1 - k), axis=0, keepdims=True))
    return total, tap_grads


def triangle(rows):
    down = lax.broadcasted_iota(jnp.int32, (rows, rows), 0)
    across = lax.broadcasted_iota(jnp.int32, (rows, rows), 1)
    return down >= across


def head_map(channels):
    channel = lax.broadcasted_iota(jnp.int32, (channels, LANES), 0)
    head = lax.broadcasted_iota(jnp.int32, (channels, LANES), 1)
    return jnp.where(channel // P_SIZE == head, 1.0, 0.0)


def decay_of(log_decay, log_decay_t, head, causal):
    gap = log_decay[:, head : head + 1] - log_decay_t[head : head + 1, :]
    return jnp.where(causal, jnp.exp(jnp.where(causal, gap, 0.0)), 0.0)


def up8(count):
    return -(-count // 8) * 8


def bits_of(size):
    return size.bit_length() - 1


def reversed_bits(value, count):
    return sum(((value >> i) & 1) << (count - 1 - i) for i in range(count))


def selection(width, bases, keep, step, shift):
    columns = len(bases) * step
    at = lax.broadcasted_iota(jnp.int32, (1, columns), 1)
    feature = at + bases[0]
    part = at
    for q in range(1, len(bases)):
        move = bases[q] - bases[q - 1] - step
        inside = at >= q * step
        feature = feature + jnp.where(inside, move, 0)
        part = part - jnp.where(inside, step, 0)
    feature = feature + shift
    if keep != step:
        feature = jnp.where(part < keep, feature, -1)
    row = lax.broadcasted_iota(jnp.int32, (width, columns), 0)
    return jnp.where(row == feature, 1.0, 0.0)


class Sizes:
    def __init__(self, dp, tensor, rows, width, channels, both, heads):
        self.dp, self.tensor = dp, tensor
        self.rows, self.width, self.channels = rows, width, channels
        self.both, self.heads = both, heads
        self.dp_bits, self.tensor_bits = bits_of(dp), bits_of(tensor)
        assert dp == 1 << self.dp_bits and tensor == 1 << self.tensor_bits
        assert self.dp_bits >= 1 and self.tensor_bits >= 1 and rows == LENGTH
        self.own = width // dp
        self.ownp = up8(self.own)
        self.blocks = dp // 2
        self.half = self.blocks * self.ownp
        self.cut = self.own // tensor
        self.cutp = up8(self.cut)
        self.shared = dp * tensor * self.cutp
        self.lanes = P_SIZE // dp
        self.piece = both // (dp * tensor)
        self.head_rows = up8(heads)
        self.small = 8 + self.head_rows


class Inputs(NamedTuple):
    tokens: Any
    cotangent: Any
    norm_gain: Any
    w_z: Any
    w_x: Any
    w_bc: Any
    w_dt: Any
    conv_x: Any
    conv_x_bias: Any
    conv_bc: Any
    conv_bc_bias: Any
    dt_bias: Any
    a_log: Any
    d_skip: Any
    gate_gain: Any
    w_out: Any


class Outputs(NamedTuple):
    output: Any
    input_grad: Any
    g_norm: Any
    g_wz: Any
    g_wx: Any
    g_wdt: Any
    g_wout: Any
    g_chan: Any
    g_wbc: Any
    g_bcc: Any
    g_heads: Any


def out_shapes(z):
    shapes = Outputs(
        output=(z.rows, z.width),
        input_grad=(z.rows, z.width),
        g_norm=(LAYERS, z.own),
        g_wz=(LAYERS, z.own, z.channels),
        g_wx=(LAYERS, z.own, z.channels),
        g_wdt=(z.heads, LAYERS, z.own),
        g_wout=(LAYERS, z.own, z.channels),
        g_chan=(K + 2, z.heads, LAYERS, z.lanes),
        g_wbc=(LAYERS, z.cut, z.both),
        g_bcc=(K + 1, LAYERS, z.piece),
        g_heads=(3, LAYERS, z.heads),
    )
    return [jax.ShapeDtypeStruct(shape, jnp.float32) for shape in shapes]


def scratch_shapes(z):
    f32, bf16 = jnp.float32, jnp.bfloat16
    rows, width, channels, both = z.rows, z.width, z.channels, z.both

    def new(*shape):
        return pltpu.VMEM(shape, f32)

    def steps(count, *shape):
        return [new(*shape) for _ in range(count)]

    def layers(make):
        return [make() for _ in range(LAYERS)]

    def halves(start, first, count, columns):
        return [new(start >> s, columns) for s in range(first, count)]

    per_sum = range(2 * LAYERS)
    return Scratch(
            wdt=pltpu.VMEM((LAYERS, LANES, width), bf16),
            hvec=new(LAYERS, 8, LANES),
            resid=new(LAYERS - 1, rows, width),
            normed=pltpu.VMEM((LAYERS, rows, width), bf16),
            zg=new(LAYERS, rows, channels),
            xi=new(LAYERS, rows, channels),
            bci=new(LAYERS, rows, both),
            dti=new(LAYERS, rows, LANES),
            y=new(LAYERS, rows, channels),
            dxdt=new(rows, channels),
            part=steps(2, rows, width),
            rowsum=[steps(z.tensor_bits, rows // 2, width) for _ in range(2)],
            rowin=steps(2 * LAYERS, rows // 2, width),
            rowx=[steps(z.tensor_bits, rows // 2, width)[1:] for _ in per_sum],
            full=steps(2, rows, width),
            stat=layers(lambda: steps(z.tensor_bits + 1, 8, rows)),
            statin=layers(lambda: steps(z.tensor_bits + 1, 8, rows)),
            to_normed=new(rows // 2, z.half),
            to_db=new(rows // 2, z.half),
            db_all=pltpu.VMEM((rows, width), bf16),
            to_gated=new(rows, channels),
            to_dzg=new(rows, channels),
            to_dxi=new(rows, channels),
            from_normed=steps(LAYERS, rows, z.half),
            from_db=steps(LAYERS, rows, z.half),
            from_gated=steps(LAYERS, rows, channels),
            from_dzg=steps(LAYERS, rows, channels),
            from_dxi=steps(LAYERS, rows, channels),
            normed_sel=pltpu.VMEM((LAYERS, rows, z.half), bf16),
            gated=pltpu.VMEM((LAYERS, rows, channels), bf16),
            sum_wout=steps(LAYERS, z.half, channels),
            sum_wz=steps(LAYERS, z.half, channels),
            sum_wx=steps(LAYERS, z.half, channels),
            in_wout=layers(lambda: halves(z.half, 1, z.dp_bits, channels)),
            in_wz=layers(lambda: halves(z.half, 1, z.dp_bits, channels)),
            in_wx=layers(lambda: halves(z.half, 1, z.dp_bits, channels)),
            sum_wbc=steps(LAYERS, z.shared, both),
            in_wbc=layers(lambda: halves(z.shared, 1, z.tensor_bits + z.dp_bits + 1, both)),
            small=layers(lambda: steps(z.dp_bits + 1, z.small, width)),
            smallin=layers(lambda: steps(z.dp_bits, z.small, width)),
            bcc=layers(lambda: steps(z.tensor_bits + 1, 8, both)),
            bccin=layers(lambda: steps(z.tensor_bits, 8, both)),
            send_sem=pltpu.SemaphoreType.DMA((COPIES,)),
            recv_sem=pltpu.SemaphoreType.DMA((COPIES,)),
    )


class Scratch(NamedTuple):
    wdt: Any
    hvec: Any
    resid: Any
    normed: Any
    zg: Any
    xi: Any
    bci: Any
    dti: Any
    y: Any
    dxdt: Any
    part: Any
    rowsum: Any
    rowin: Any
    rowx: Any
    full: Any
    stat: Any
    statin: Any
    to_normed: Any
    to_db: Any
    db_all: Any
    to_gated: Any
    to_dzg: Any
    to_dxi: Any
    from_normed: Any
    from_db: Any
    from_gated: Any
    from_dzg: Any
    from_dxi: Any
    normed_sel: Any
    gated: Any
    sum_wout: Any
    sum_wz: Any
    sum_wx: Any
    in_wout: Any
    in_wz: Any
    in_wx: Any
    sum_wbc: Any
    in_wbc: Any
    small: Any
    smallin: Any
    bcc: Any
    bccin: Any
    send_sem: Any
    recv_sem: Any


COPIES = 128
SCAN = jnp.bfloat16


def scan_dot(left, right, dims=((1,), (0,))):
    return matmul(left, right, dims, HIGHEST_PREC if SCAN == jnp.float32 else None)


class Flow:
    def __init__(self, z, r):
        self.z, self.r = z, r
        self.at = {DP: lax.axis_index(DP), TENSOR: lax.axis_index(TENSOR)}
        self.copies = []
        self.leaving = {}
        self.done = set()

    def bit(self, axis, bit):
        return lax.rem(lax.div(self.at[axis], 1 << bit), 2)

    def peer(self, axis, bit):
        there = dict(self.at)
        there[axis] = self.at[axis] + (1 << bit) * (1 - 2 * self.bit(axis, bit))
        return (there[DP], there[TENSOR])

    def every(self, axis):
        count = self.z.dp_bits if axis == DP else self.z.tensor_bits
        return [(axis, b) for b in range(count)]

    def barrier(self):
        everyone = self.every(DP) + self.every(TENSOR)
        barrier = pltpu.get_barrier_semaphore()
        for axis, bit in everyone:
            pl.semaphore_signal(
                barrier, inc=1, device_id=self.peer(axis, bit), device_id_type=MESH
            )
        pl.semaphore_wait(barrier, len(everyone))

    def release(self, key):
        index = self.leaving.pop(key, None)
        if index is not None:
            self.copies[index].wait_send()
            self.done.add(index)

    def send(self, source, target, axis, bit, key=None):
        index = len(self.copies)
        if key is not None:
            self.leaving[key] = index
        copy = pltpu.make_async_remote_copy(
            src_ref=source,
            dst_ref=target,
            send_sem=self.r.send_sem.at[index],
            recv_sem=self.r.recv_sem.at[index],
            device_id=self.peer(axis, bit),
            device_id_type=MESH,
        )
        copy.start()
        self.copies.append(copy)
        return copy

    def drain(self):
        for index, copy in enumerate(self.copies):
            if index not in self.done:
                copy.wait_send()

    def half(self, which):
        count = self.z.rows // 2
        return pl.ds(pl.multiple_of(which * count, 16), count)

    def factor(self, source, landing, value):
        self.release(id(source))
        source[...] = value
        return self.send(source, landing, DP, 0, id(source))

    def shared_factor(self, source, landing, value):
        mine = self.half(self.bit(TENSOR, 0))
        self.release(id(source))
        source[...] = value
        copy = self.send(source, landing.at[mine], DP, 0, id(source))
        yield
        copy.wait_recv()
        copy = self.send(landing.at[mine], landing.at[mine], TENSOR, 0)
        yield
        copy.wait_recv()

    def row_sum(self, k, value, full):
        r = self.r
        bit = self.bit(TENSOR, 0)
        here, there = self.half(bit), self.half(1 - bit)
        slot = k % 2
        part = r.part[slot]
        self.release(id(part))
        part[...] = value
        copy = self.send(part.at[there], r.rowin[k], TENSOR, 0, id(part))
        yield
        copy.wait_recv()
        total = part[here, :] + r.rowin[k][...]
        for s in range(1, self.z.tensor_bits):
            held = r.rowsum[slot][s]
            self.release(id(held))
            held[...] = total
            copy = self.send(held, r.rowx[k][s - 1], TENSOR, s, id(held))
            yield
            copy.wait_recv()
            total = held[...] + r.rowx[k][s - 1][...]
        full[here, :] = total
        copy = self.send(full.at[here], full.at[here], TENSOR, 0, id(full))
        yield
        copy.wait_recv()

    def scatter(self, buffer, landings, bits, finish):
        count, low = buffer.shape[0], 0
        for (axis, bit), landing in zip(bits, landings, strict=True):
            count //= 2
            mine = self.bit(axis, bit)
            keep = pl.multiple_of(low + mine * count, 8)
            give = pl.multiple_of(low + (1 - mine) * count, 8)
            copy = self.send(buffer.at[pl.ds(give, count)], landing, axis, bit)
            yield
            copy.wait_recv()
            buffer[pl.ds(keep, count), :] += landing[...]
            low = keep
        finish(buffer[pl.ds(low, count), :])

    def butterfly(self, held, landings, bits):
        for s, (axis, bit) in enumerate(bits):
            copy = self.send(held[s], landings[s], axis, bit)
            yield
            copy.wait_recv()
            held[s + 1][...] = held[s][...] + landings[s][...]


def drive(task):
    for _ in task:
        pass


def step(*tasks):
    for task in tasks:
        next(task, None)


def fused_kernel(z, *refs):
    ins, outs = len(Inputs._fields), len(Outputs._fields)
    r = SimpleNamespace(
        **Inputs(*refs[:ins])._asdict(),
        **Outputs(*refs[ins : ins + outs])._asdict(),
        **Scratch(*refs[ins + outs :])._asdict(),
    )
    flow = Flow(z, r)
    rows, width, channels, both, heads = z.rows, z.width, z.channels, z.both, z.heads
    inner = channels * z.tensor
    bf16, f32 = jnp.bfloat16, jnp.float32
    dp_at, tensor_at = flow.at[DP], flow.at[TENSOR]
    parity = flow.bit(DP, 0)
    my_rows = flow.half(flow.bit(TENSOR, 0))
    last = LAYERS - 1

    flow.barrier()

    bases = [2 * reversed_bits(q, z.dp_bits - 1) * z.own for q in range(z.blocks)]
    pick_other = selection(width, bases, z.own, z.ownp, (1 - parity) * z.own).astype(bf16)
    shared_bases = [
        reversed_bits(p, z.dp_bits) * z.own + reversed_bits(t, z.tensor_bits) * z.cut
        for t in range(z.tensor)
        for p in range(z.dp)
    ]

    def pick_shared(t):
        group = shared_bases[t * z.dp : (t + 1) * z.dp]
        return selection(width, group, z.cut, z.cutp, 0).astype(bf16)

    cot_task = flow.shared_factor(
        r.to_db, r.from_db[last], matmul(r.cotangent[my_rows, :], pick_other)
    )
    step(cot_task)
    pick_mine = selection(width, bases, z.own, z.ownp, parity * z.own).astype(bf16)
    full = [r.full[0], r.output, r.full[1], r.input_grad]

    for l in range(LAYERS):
        given = [r.w_dt[head].astype(f32)[l : l + 1, :] for head in range(heads)]
        given.append(jnp.zeros((LANES - heads, width), f32))
        r.wdt[l] = jnp.concatenate(given, axis=0).astype(bf16)
        r.hvec[l] = jnp.zeros((8, LANES), f32)
        r.hvec[l, 0:1, :heads] = r.a_log[l : l + 1, :]
        r.hvec[l, 1:2, :heads] = r.d_skip[l : l + 1, :]
        r.hvec[l, 2:3, :heads] = r.dt_bias[l : l + 1, :]

    causal = triangle(rows)
    lower = jnp.where(causal, 1.0, 0.0)
    spread = head_map(channels)
    ones = jnp.ones((8, width), f32)
    eye = jnp.where(
        lax.broadcasted_iota(jnp.int32, (rows, rows), 0)
        == lax.broadcasted_iota(jnp.int32, (rows, rows), 1),
        1.0,
        0.0,
    )
    stat_row = lax.broadcasted_iota(jnp.int32, (8, rows), 0)
    factors = {}

    def column(stat):
        return exact(eye, stat, COLS_COLS)

    def residual(l):
        return r.tokens[...].astype(f32) if l == 0 else r.resid[l - 1]

    def forward(l):
        h = residual(l)
        scale = lax.rsqrt(jnp.mean(h * h, axis=1, keepdims=True) + EPSILON)
        normed = (h * scale * r.norm_gain[l : l + 1, :]).astype(bf16)
        r.normed[l] = normed
        normed_task = flow.shared_factor(
            r.to_normed, r.from_normed[l], matmul(r.normed[l, my_rows, :], pick_other)
        )
        step(normed_task)
        zg = matmul(normed, r.w_z[l])
        xi = matmul(normed, r.w_x[l])
        bci = matmul(normed, r.w_bc[l])
        dti = matmul(normed, r.wdt[l], COLS_COLS)
        r.zg[l] = zg
        r.xi[l] = xi
        r.bci[l] = bci
        r.dti[l] = dti
        hvec = r.hvec[l]
        pre_x = causal_conv(xi, r.conv_x[l], r.conv_x_bias[l : l + 1, :])
        xc = pre_x * sigmoid(pre_x)
        pre_b = causal_conv(bci, r.conv_bc[l], r.conv_bc_bias[l : l + 1, :])
        bcc = pre_b * sigmoid(pre_b)
        state = both // 2
        dt = softplus(dti + hvec[2:3, :])
        rate = -jnp.exp(hvec[0:1, :]) * dt
        log_decay = exact(lower, rate)
        log_decay_t = exact(rate, lower, ((0,), (1,)))
        xdt = (xc * exact(dt, spread, COLS_COLS)).astype(SCAN)
        scores = scan_dot(bcc[:, state:].astype(SCAN), bcc[:, :state].astype(SCAN), COLS_COLS)
        for head in range(heads):
            cols = slice(head * P_SIZE, (head + 1) * P_SIZE)
            weights = scores * decay_of(log_decay, log_decay_t, head, causal)
            r.y[l, :, cols] = scan_dot(weights.astype(SCAN), xdt[:, cols])
        y = r.y[l] + exact(hvec, spread, COLS_COLS)[1:2, :] * xc
        core = y * (zg * sigmoid(zg))
        gated = (core * r.gate_gain[l : l + 1, :]).astype(bf16)
        partial = matmul(gated, r.w_out[l])
        sum_task = flow.row_sum(l, partial, full[l])
        step(sum_task)
        stat = jnp.where(stat_row == 0, exact(ones[:, :channels], core * core, COLS_COLS), 0.0)
        if l == last:
            product = exact(ones, r.cotangent[...].astype(f32) * partial, COLS_COLS)
            stat = jnp.where(stat_row == 1, product, stat)
        r.stat[l][0][...] = stat
        stat_task = flow.butterfly(r.stat[l], r.statin[l], flow.every(TENSOR))
        step(stat_task)
        r.gated[l] = gated
        copy = flow.factor(r.to_gated, r.from_gated[l], gated.astype(f32))
        if l < last:
            step(sum_task)
        step(stat_task)
        r.normed_sel[l] = matmul(normed, pick_mine).astype(bf16)
        drive(stat_task)
        stat = column(r.stat[l][z.tensor_bits][...])
        factors[l] = (lax.rsqrt(stat[:, 0:1] / inner + EPSILON), stat[:, 1:2])
        return sum_task, normed_task, copy

    gated_copies, normed_tasks = {}, {}
    for l in range(LAYERS):
        sum_task, normed_tasks[l], gated_copies[l] = forward(l)
        if l < last:
            step(cot_task, normed_tasks[l])
            drive(sum_task)
            r.resid[l] = residual(l) + factors[l][0] * full[l][...]

    output_task = sum_task
    statistic = flow.send(r.stat[last][z.tensor_bits], r.statin[last][z.tensor_bits], DP, 0)
    sums = {"o": (r.sum_wout, r.in_wout), "z": (r.sum_wz, r.in_wz), "x": (r.sum_wx, r.in_wx)}
    owned = {"o": r.g_wout, "z": r.g_wz, "x": r.g_wx, "b": r.g_wbc}
    tasks = {}

    def finish_to(m, l, count):
        def finish(value):
            owned[m][l] = value[:count, :]

        return finish

    def start_scatter(m, l, value):
        total, landings = sums[m]
        total[l][...] = value
        bits = flow.every(DP)[1:]
        tasks[m, l] = flow.scatter(total[l], landings[l], bits, finish_to(m, l, z.own))
        step(tasks[m, l])

    def weight_product(m, l, copy):
        sent, landing = {"z": (r.to_dzg, r.from_dzg), "x": (r.to_dxi, r.from_dxi)}[m]
        own = matmul(r.normed_sel[l], sent[...].astype(bf16), ROWS_ROWS)
        copy.wait_recv()
        theirs = matmul(
            r.from_normed[l][...].astype(bf16), landing[l][...].astype(bf16), ROWS_ROWS
        )
        start_scatter(m, l, own + theirs)

    def wout_product(l, db, their_db):
        own = matmul(matmul(db, pick_mine).astype(bf16), r.gated[l], ROWS_ROWS)
        theirs = matmul(their_db, r.from_gated[l][...].astype(bf16), ROWS_ROWS)
        start_scatter("o", l, own + theirs)

    def small_task(l):
        yield from flow.butterfly(r.small[l], r.smallin[l], flow.every(DP))
        small = r.small[l][z.dp_bits][...]
        r.bcc[l][0][...] = small[0:8, width - both :]
        pick = selection(width, [0], z.own, z.own, dp_at * z.own)
        r.g_norm[l : l + 1, :] = exact(small[0:8, :], pick)[6:7, :]
        by_head = exact(small[8:, :], pick)
        for head in range(heads):
            r.g_wdt[head, l : l + 1, :] = by_head[head : head + 1, :]
            pick = selection(channels, [0], z.lanes, z.lanes, head * P_SIZE + dp_at * z.lanes)
            chan = exact(small[0:8, :channels], pick)
            for row in range(K + 2):
                r.g_chan[row, head, l : l + 1, :] = chan[row : row + 1, :]
        for row in range(3):
            r.g_heads[row, l : l + 1, :] = small[row : row + 1, channels : channels + heads]
        yield from flow.butterfly(r.bcc[l], r.bccin[l], flow.every(TENSOR))
        pick = selection(both, [0], z.piece, z.piece, (dp_at * z.tensor + tensor_at) * z.piece)
        bcc = exact(r.bcc[l][z.tensor_bits][...], pick)
        for row in range(K + 1):
            r.g_bcc[row, l : l + 1, :] = bcc[row : row + 1, :]

    copies = {}

    def backward(l, g):
        f, product = factors[l]
        normed = r.normed[l]
        db = (g * f).astype(bf16)
        if l != last:
            r.db_all[...] = db
            db_task = flow.shared_factor(
                r.to_db, r.from_db[l], matmul(r.db_all[my_rows, :], pick_other)
            )
            step(db_task)
            product = jnp.sum(g * full[l][...], axis=1, keepdims=True)
        small = r.small[l][0]
        small[...] = jnp.zeros_like(small)
        zg = r.zg[l]
        xi = r.xi[l]
        hvec = r.hvec[l]
        skip = exact(hvec, spread, COLS_COLS)[1:2, :]
        taps_x = r.conv_x[l]
        taps_b = r.conv_bc[l]
        pre_x = causal_conv(xi, taps_x, r.conv_x_bias[l : l + 1, :])
        sx = sigmoid(pre_x)
        xc = pre_x * sx
        within = r.y[l]
        y = within + skip * xc
        gate = r.gate_gain[l : l + 1, :]
        sz = sigmoid(zg)
        silu = zg * sz
        core = y * silu
        dgated = matmul(db, r.w_out[l], COLS_COLS)
        dms = -0.5 * f * f * f * product
        small[K + 1 : K + 2, :channels] = jnp.sum(dgated * core, axis=0, keepdims=True)
        dcore = dgated * gate + dms * (2.0 / inner) * core
        dy = dcore * silu
        dzg = (dcore * y * (sz * (1.0 + zg * (1.0 - sz)))).astype(bf16)
        copies["z", l] = flow.factor(r.to_dzg, r.from_dzg[l], dzg.astype(f32))
        back = matmul(dzg, r.w_z[l], COLS_COLS)

        if l == last:
            step(output_task)
            step(normed_tasks[last])
            drive(cot_task)
            drive(normed_tasks[0])
        else:
            weight_product("x", last, copies["x", last])
            step(tasks["b", last])
            step(tasks["s", last])

        bci = r.bci[l]
        dti = r.dti[l]
        pre_b = causal_conv(bci, taps_b, r.conv_bc_bias[l : l + 1, :])
        sb = sigmoid(pre_b)
        bcc = pre_b * sb
        state = both // 2
        keys = bcc[:, :state].astype(SCAN)
        queries = bcc[:, state:].astype(SCAN)
        raw = dti + hvec[2:3, :]
        dt = softplus(raw)
        neg = -jnp.exp(hvec[0:1, :])
        rate = neg * dt
        log_decay = exact(lower, rate)
        log_decay_t = exact(rate, lower, ((0,), (1,)))
        dt_full = exact(dt, spread, COLS_COLS)
        xdt = (xc * dt_full).astype(SCAN)
        dys = dy.astype(SCAN)
        scores = scan_dot(queries, keys, COLS_COLS)
        dscores = jnp.zeros_like(scores)
        for head in range(heads):
            cols = slice(head * P_SIZE, (head + 1) * P_SIZE)
            decay = decay_of(log_decay, log_decay_t, head, causal)
            dy_h = dys[:, cols]
            dscores = dscores + scan_dot(dy_h, xdt[:, cols], COLS_COLS) * decay
            r.dxdt[:, cols] = scan_dot((scores * decay).astype(SCAN), dy_h, ROWS_ROWS)
        dxdt = r.dxdt[...]

        dpre_x = (dxdt * dt_full + skip * dy) * (sx * (1.0 + pre_x * (1.0 - sx)))
        dxi, tap_grads = conv_back(xi, taps_x, dpre_x)
        for k in range(K):
            small[k : k + 1, :channels] = tap_grads[k]
        small[K : K + 1, :channels] = jnp.sum(dpre_x, axis=0, keepdims=True)
        dxi = dxi.astype(bf16)
        copies["x", l] = flow.factor(r.to_dxi, r.from_dxi[l], dxi.astype(f32))
        back = back + matmul(dxi, r.w_x[l], COLS_COLS)

        if l == last:
            drive(normed_tasks[last])
            gated_copies[0].wait_recv()
            gated_copies[last].wait_recv()
            statistic.wait_recv()
            stat = column(r.statin[last][z.tensor_bits][...])
            their_f = lax.rsqrt(stat[:, 0:1] / inner + EPSILON)
            wout_product(l, db, (r.from_db[l][...] * their_f).astype(bf16))
        else:
            step(db_task)
            step(tasks["o", last])
            step(tasks["b", last])
            step(tasks["s", last])
            step(tasks["z", last])

        dlog = exact(dys.astype(f32) * within - xdt.astype(f32) * dxdt, spread)
        drate = exact(lower, dlog, ROWS_ROWS)
        ddt = exact(dxdt * xc, spread) + drate * neg
        draw = ddt * sigmoid(raw)
        at = slice(channels, channels + LANES)
        small[0:1, at] = jnp.sum(drate * rate, axis=0, keepdims=True)
        small[1:2, at] = jnp.sum(exact(dy * xc, spread), axis=0, keepdims=True)
        small[2:3, at] = jnp.sum(draw, axis=0, keepdims=True)
        ddti = draw.astype(bf16)
        small[8:, :] = matmul(ddti, normed, ROWS_ROWS)[: z.head_rows, :]
        back = back + matmul(ddti, r.wdt[l])

        dscores = dscores.astype(SCAN)
        dkeys = scan_dot(dscores, queries, ROWS_ROWS)
        dqueries = scan_dot(dscores, keys)
        dbcc = jnp.concatenate([dkeys, dqueries], axis=1)
        dpre_b = dbcc * (sb * (1.0 + pre_b * (1.0 - sb)))
        dbci, tap_grads = conv_back(bci, taps_b, dpre_b)
        for k in range(K):
            small[k : k + 1, width - both :] = tap_grads[k]
        small[K : K + 1, width - both :] = jnp.sum(dpre_b, axis=0, keepdims=True)
        dbci = dbci.astype(bf16)
        k = 2 * LAYERS - 1 - l
        back = back + matmul(dbci, r.w_bc[l], COLS_COLS)
        back_task = flow.row_sum(k, back, full[k])
        step(back_task)
        if l == last:
            step(output_task)
        for t in range(z.tensor):
            picked = matmul(normed, pick_shared(t)).astype(bf16)
            group = z.dp * z.cutp
            r.sum_wbc[l][t * group : (t + 1) * group, :] = matmul(picked, dbci, ROWS_ROWS)
        step(back_task)

        bits = flow.every(TENSOR) + flow.every(DP)
        tasks["b", l] = flow.scatter(
            r.sum_wbc[l], r.in_wbc[l], bits, finish_to("b", l, z.cut)
        )
        step(tasks["b", l])
        if l == last:
            weight_product("z", l, copies["z", l])
            drive(output_task)
            flow.release(id(r.output))
            r.output[...] = residual(l) + f * r.output[...]
        else:
            drive(db_task)
            wout_product(l, db, r.from_db[l][...].astype(bf16))
            step(tasks["b", last])
            step(tasks["s", last])
            weight_product("z", l, copies["z", l])
        step(tasks["b", l])
        drive(back_task)

        h = residual(l)
        back_normed = full[k][...]
        scale = lax.rsqrt(jnp.mean(h * h, axis=1, keepdims=True) + EPSILON)
        small[6:7, :] = jnp.sum(back_normed * h * scale, axis=0, keepdims=True)
        tasks["s", l] = small_task(l)
        step(tasks["s", l])
        hat = back_normed * r.norm_gain[l : l + 1, :]
        return g + scale * hat - scale * scale * scale * h * jnp.mean(
            hat * h, axis=1, keepdims=True
        )

    g = r.cotangent[...].astype(f32)
    for l in reversed(range(LAYERS)):
        g = backward(l, g)
    flow.release(id(r.input_grad))
    r.input_grad[...] = g
    step(tasks["x", last])
    weight_product("x", 0, copies["x", 0])
    pending = [tasks[m, l] for l in (last, 0) for m in "sbozx"]
    while pending:
        left = []
        for task in pending:
            if next(task, pending) is not pending:
                left.append(task)
        pending = left
    flow.drain()


def deliver_kernel(count, *refs):
    for i in range(count):
        refs[count + i][...] = refs[i][...]


def on_device(dp_size, tensor_size, *args):
    given = Inputs(*args)
    rows, width = given.tokens.shape
    z = Sizes(
        dp_size,
        tensor_size,
        rows,
        width,
        given.w_z.shape[2],
        given.w_bc.shape[2],
        given.w_dt.shape[2],
    )
    given = given._replace(w_dt=jnp.transpose(given.w_dt, (2, 0, 1)))
    outs = out_shapes(z)
    results = pl.pallas_call(
        functools.partial(fused_kernel, z),
        out_shape=outs,
        in_specs=[pl.BlockSpec(memory_space=pltpu.VMEM)] * len(args),
        out_specs=[pl.BlockSpec(memory_space=pltpu.VMEM)] * len(outs),
        scratch_shapes=list(scratch_shapes(z)),
        compiler_params=pltpu.CompilerParams(
            collective_id=0, has_side_effects=True, vmem_limit_bytes=63 * 1024 * 1024
        ),
    )(*given)
    results = pl.pallas_call(
        functools.partial(deliver_kernel, len(outs)),
        out_shape=outs,
        in_specs=[pl.BlockSpec(memory_space=pltpu.VMEM)] * len(outs),
        out_specs=[pl.BlockSpec(memory_space=pltpu.VMEM)] * len(outs),
    )(*results)
    done = Outputs(*results)
    return tuple(
        done._replace(
            g_wdt=jnp.transpose(done.g_wdt, (1, 2, 0)),
            g_wout=jnp.swapaxes(done.g_wout, 1, 2),
            g_chan=jnp.transpose(done.g_chan, (2, 0, 1, 3)),
            g_bcc=jnp.swapaxes(done.g_bcc, 0, 1),
            g_heads=jnp.swapaxes(done.g_heads, 0, 1),
        )
    )


def solution(mesh):
    placed = (
        P(DP, None),
        P(DP, None),
        P(),
        P(None, None, TENSOR),
        P(None, None, TENSOR),
        P(),
        P(None, None, TENSOR),
        P(None, None, TENSOR),
        P(None, TENSOR),
        P(),
        P(),
        P(None, TENSOR),
        P(None, TENSOR),
        P(None, TENSOR),
        P(None, TENSOR),
        P(None, TENSOR, None),
    )
    return jax.shard_map(
        functools.partial(on_device, mesh.shape[DP], mesh.shape[TENSOR]),
        mesh=mesh,
        in_specs=placed,
        out_specs=(
            P(DP, None),
            P(DP, None),
            P(None, DP),
            P(None, DP, TENSOR),
            P(None, DP, TENSOR),
            P(None, DP, TENSOR),
            P(None, TENSOR, DP),
            P(None, None, TENSOR, DP),
            P(None, (DP, TENSOR), None),
            P(None, None, (DP, TENSOR)),
            P(None, None, TENSOR),
        ),
        check_vma=False,
    )
```

```python
import functools
from types import SimpleNamespace
from typing import Any, NamedTuple

import jax
import jax.numpy as jnp
from jax import lax
from jax.experimental import pallas as pl
from jax.experimental.pallas import tpu as pltpu
from jax.sharding import PartitionSpec as P

P_SIZE = 64
K = 4
LANES = 128
DP, TENSOR = "dp", "tensor"
LENGTH = 256
LAYERS = 2
EPSILON = 1e-05
HIGHEST_PREC = lax.Precision.HIGHEST
MESH = pl.DeviceIdType.MESH
ROWS_ROWS = ((0,), (0,))
COLS_COLS = ((1,), (1,))


def matmul(left, right, dims=((1,), (0,)), precision=None):
    return lax.dot_general(
        left, right, (dims, ((), ())), precision=precision, preferred_element_type=jnp.float32
    )


def exact(left, right, dims=((1,), (0,))):
    return matmul(left, right, dims, HIGHEST_PREC)


def sigmoid(value):
    return 1.0 / (1.0 + jnp.exp(-value))


def softplus(value):
    return jnp.maximum(value, 0.0) + jnp.log1p(jnp.exp(-jnp.abs(value)))


def delayed(signal, shift):
    if shift == 0:
        return signal
    rows = signal.shape[0]
    moved = pltpu.roll(signal, shift % rows, 0)
    at = lax.broadcasted_iota(jnp.int32, signal.shape, 0)
    inside = at >= shift if shift > 0 else at < rows + shift
    return jnp.where(inside, moved, 0.0)


def causal_conv(signal, taps, offset):
    total = offset
    for k in range(K):
        total = total + taps[k : k + 1, :] * delayed(signal, K - 1 - k)
    return total


def conv_back(taps, back):
    total = jnp.zeros_like(back)
    for k in range(K):
        total = total + taps[k : k + 1, :] * delayed(back, k + 1 - K)
    return total


def triangle(rows):
    down = lax.broadcasted_iota(jnp.int32, (rows, rows), 0)
    across = lax.broadcasted_iota(jnp.int32, (rows, rows), 1)
    return down >= across


def head_map(channels):
    channel = lax.broadcasted_iota(jnp.int32, (channels, LANES), 0)
    head = lax.broadcasted_iota(jnp.int32, (channels, LANES), 1)
    return jnp.where(channel // P_SIZE == head, 1.0, 0.0)


def decay_of(log_decay, log_decay_t, head, causal):
    gap = log_decay[:, head : head + 1] - log_decay_t[head : head + 1, :]
    return jnp.where(causal, jnp.exp(jnp.where(causal, gap, 0.0)), 0.0)


def up8(count):
    return -(-count // 8) * 8


def bits_of(size):
    return size.bit_length() - 1


def reversed_bits(value, count):
    return sum(((value >> i) & 1) << (count - 1 - i) for i in range(count))


def selection(width, bases, keep, step, shift):
    columns = len(bases) * step
    at = lax.broadcasted_iota(jnp.int32, (1, columns), 1)
    feature = at + bases[0]
    part = at
    for q in range(1, len(bases)):
        move = bases[q] - bases[q - 1] - step
        inside = at >= q * step
        feature = feature + jnp.where(inside, move, 0)
        part = part - jnp.where(inside, step, 0)
    feature = feature + shift
    if keep != step:
        feature = jnp.where(part < keep, feature, -1)
    row = lax.broadcasted_iota(jnp.int32, (width, columns), 0)
    return jnp.where(row == feature, 1.0, 0.0)


class Sizes:
    def __init__(self, dp, tensor, rows, width, channels, both, heads):
        self.dp, self.tensor = dp, tensor
        self.rows, self.width, self.channels = rows, width, channels
        self.both, self.heads = both, heads
        self.dp_bits, self.tensor_bits = bits_of(dp), bits_of(tensor)
        assert dp == 1 << self.dp_bits and tensor == 1 << self.tensor_bits
        assert self.dp_bits >= 1 and self.tensor_bits >= 1 and rows == LENGTH
        self.own = width // dp
        self.ownp = up8(self.own)
        self.blocks = dp // 2
        self.half = self.blocks * self.ownp
        self.cut = self.own // tensor
        self.cutp = up8(self.cut)
        self.shared = dp * tensor * self.cutp
        self.lanes = P_SIZE // dp
        self.piece = both // (dp * tensor)
        self.head_rows = up8(heads)
        self.small = 8 + self.head_rows


class Inputs(NamedTuple):
    tokens: Any
    cotangent: Any
    norm_gain: Any
    w_z: Any
    w_x: Any
    w_bc: Any
    w_dt: Any
    conv_x: Any
    conv_x_bias: Any
    conv_bc: Any
    conv_bc_bias: Any
    dt_bias: Any
    a_log: Any
    d_skip: Any
    gate_gain: Any
    w_out: Any


class Outputs(NamedTuple):
    output: Any
    input_grad: Any
    g_norm: Any
    g_wz: Any
    g_wx: Any
    g_wdt: Any
    g_wout: Any
    g_chan: Any
    g_wbc: Any
    g_bcc: Any
    g_heads: Any


def out_shapes(z):
    shapes = Outputs(
        output=(z.rows, z.width),
        input_grad=(z.rows, z.width),
        g_norm=(LAYERS, z.own),
        g_wz=(LAYERS, z.own, z.channels),
        g_wx=(LAYERS, z.own, z.channels),
        g_wdt=(z.heads, LAYERS, z.own),
        g_wout=(LAYERS, z.own, z.channels),
        g_chan=(K + 2, z.heads, LAYERS, z.lanes),
        g_wbc=(LAYERS, z.cut, z.both),
        g_bcc=(K + 1, LAYERS, z.piece),
        g_heads=(3, LAYERS, z.heads),
    )
    return [jax.ShapeDtypeStruct(shape, jnp.float32) for shape in shapes]


def scratch_shapes(z):
    f32, bf16 = jnp.float32, jnp.bfloat16
    rows, width, channels, both = z.rows, z.width, z.channels, z.both

    def new(*shape):
        return pltpu.VMEM(shape, f32)

    def steps(count, *shape):
        return [new(*shape) for _ in range(count)]

    def layers(make):
        return [make() for _ in range(LAYERS)]

    def halves(start, first, count, columns):
        return [new(start >> s, columns) for s in range(first, count)]

    per_sum = range(2 * LAYERS)
    return Scratch(
            wdt=pltpu.VMEM((LAYERS, LANES, width), bf16),
            hvec=new(LAYERS, 8, LANES),
            resid=new(LAYERS - 1, rows, width),
            normed=pltpu.VMEM((LAYERS, rows, width), bf16),
            zg=new(LAYERS, rows, channels),
            xi=new(LAYERS, rows, channels),
            bci=new(LAYERS, rows, both),
            dti=new(LAYERS, rows, LANES),
            y=new(LAYERS, rows, channels),
            dxdt=new(rows, channels),
            part=steps(2, rows, width),
            rowsum=[steps(z.tensor_bits, rows // 2, width) for _ in range(2)],
            rowin=steps(2 * LAYERS, rows // 2, width),
            rowx=[steps(z.tensor_bits, rows // 2, width)[1:] for _ in per_sum],
            full=steps(2, rows, width),
            stat=layers(lambda: steps(z.tensor_bits + 1, 8, rows)),
            statin=layers(lambda: steps(z.tensor_bits + 1, 8, rows)),
            to_normed=new(rows // 2, z.half),
            to_db=new(rows // 2, z.half),
            db_all=pltpu.VMEM((rows, width), bf16),
            to_gated=new(rows, channels),
            to_dzg=new(rows, channels),
            to_dxi=new(rows, channels),
            from_normed=steps(LAYERS, rows, z.half),
            from_db=steps(LAYERS, rows, z.half),
            from_gated=steps(LAYERS, rows, channels),
            from_dzg=steps(LAYERS, rows, channels),
            from_dxi=steps(LAYERS, rows, channels),
            normed_sel=pltpu.VMEM((LAYERS, rows, z.half), bf16),
            gated=pltpu.VMEM((LAYERS, rows, channels), bf16),
            sum_wout=steps(LAYERS, z.half, channels),
            sum_wz=steps(LAYERS, z.half, channels),
            sum_wx=steps(LAYERS, z.half, channels),
            in_wout=layers(lambda: halves(z.half, 1, z.dp_bits, channels)),
            in_wz=layers(lambda: halves(z.half, 1, z.dp_bits, channels)),
            in_wx=layers(lambda: halves(z.half, 1, z.dp_bits, channels)),
            sum_wbc=steps(LAYERS, z.shared, both),
            in_wbc=layers(lambda: halves(z.shared, 1, z.tensor_bits + z.dp_bits + 1, both)),
            small=layers(lambda: steps(z.dp_bits + 1, z.small, width)),
            smallin=layers(lambda: steps(z.dp_bits, z.small, width)),
            bcc=layers(lambda: steps(z.tensor_bits + 1, 8, both)),
            bccin=layers(lambda: steps(z.tensor_bits, 8, both)),
            send_sem=pltpu.SemaphoreType.DMA((COPIES,)),
            recv_sem=pltpu.SemaphoreType.DMA((COPIES,)),
    )


class Scratch(NamedTuple):
    wdt: Any
    hvec: Any
    resid: Any
    normed: Any
    zg: Any
    xi: Any
    bci: Any
    dti: Any
    y: Any
    dxdt: Any
    part: Any
    rowsum: Any
    rowin: Any
    rowx: Any
    full: Any
    stat: Any
    statin: Any
    to_normed: Any
    to_db: Any
    db_all: Any
    to_gated: Any
    to_dzg: Any
    to_dxi: Any
    from_normed: Any
    from_db: Any
    from_gated: Any
    from_dzg: Any
    from_dxi: Any
    normed_sel: Any
    gated: Any
    sum_wout: Any
    sum_wz: Any
    sum_wx: Any
    in_wout: Any
    in_wz: Any
    in_wx: Any
    sum_wbc: Any
    in_wbc: Any
    small: Any
    smallin: Any
    bcc: Any
    bccin: Any
    send_sem: Any
    recv_sem: Any


COPIES = 160
CHUNKS = 2
SCAN = jnp.bfloat16


def scan_dot(left, right, dims=((1,), (0,))):
    return matmul(left, right, dims, HIGHEST_PREC if SCAN == jnp.float32 else None)


class Flow:
    def __init__(self, z, r):
        self.z, self.r = z, r
        self.at = {DP: lax.axis_index(DP), TENSOR: lax.axis_index(TENSOR)}
        self.copies = []
        self.leaving = {}
        self.done = set()

    def bit(self, axis, bit):
        return lax.rem(lax.div(self.at[axis], 1 << bit), 2)

    def peer(self, axis, bit):
        there = dict(self.at)
        there[axis] = self.at[axis] + (1 << bit) * (1 - 2 * self.bit(axis, bit))
        return (there[DP], there[TENSOR])

    def every(self, axis):
        count = self.z.dp_bits if axis == DP else self.z.tensor_bits
        return [(axis, b) for b in range(count)]

    def barrier(self):
        everyone = self.every(DP) + self.every(TENSOR)
        barrier = pltpu.get_barrier_semaphore()
        for axis, bit in everyone:
            pl.semaphore_signal(
                barrier, inc=1, device_id=self.peer(axis, bit), device_id_type=MESH
            )
        pl.semaphore_wait(barrier, len(everyone))

    def release(self, key):
        index = self.leaving.pop(key, None)
        if index is not None:
            self.copies[index].wait_send()
            self.done.add(index)

    def send(self, source, target, axis, bit, key=None):
        index = len(self.copies)
        if key is not None:
            self.leaving[key] = index
        copy = pltpu.make_async_remote_copy(
            src_ref=source,
            dst_ref=target,
            send_sem=self.r.send_sem.at[index],
            recv_sem=self.r.recv_sem.at[index],
            device_id=self.peer(axis, bit),
            device_id_type=MESH,
        )
        copy.start()
        self.copies.append(copy)
        return copy

    def drain(self):
        for index, copy in enumerate(self.copies):
            if index not in self.done:
                copy.wait_send()

    def half(self, which):
        count = self.z.rows // 2
        return pl.ds(pl.multiple_of(which * count, 16), count)

    def factor(self, source, landing, value, bit):
        self.release(id(source))
        source[...] = value
        return self.send(source, landing, DP, bit, id(source))

    def shared_factor(self, source, landing, value, bit):
        mine = self.half(self.bit(TENSOR, 0))
        self.release(id(source))
        source[...] = value
        copy = self.send(source, landing.at[mine], DP, bit, id(source))
        yield
        copy.wait_recv()
        copy = self.send(landing.at[mine], landing.at[mine], TENSOR, 0)
        yield
        copy.wait_recv()

    def row_sum(self, k, value, full):
        r = self.r
        bit = self.bit(TENSOR, 0)
        here, there = self.half(bit), self.half(1 - bit)
        slot = k % 2
        part = r.part[slot]
        width = part.shape[1] // CHUNKS
        chunks = [pl.ds(i * width, width) for i in range(CHUNKS)]
        for i in range(CHUNKS):
            self.release((id(part), i))
        part[...] = value
        copies = [
            self.send(part.at[there, c], r.rowin[k].at[:, c], TENSOR, 0, (id(part), i))
            for i, c in enumerate(chunks)
        ]
        yield
        for s in range(self.z.tensor_bits):
            for i, c in enumerate(chunks):
                copies[i].wait_recv()
                if s == 0:
                    total = part[here, c] + r.rowin[k][:, c]
                else:
                    total = r.rowsum[slot][s][:, c] + r.rowx[k][s - 1][:, c]
                if s == self.z.tensor_bits - 1:
                    full[here, c] = total
                    target = full.at[here, c]
                    copies[i] = self.send(target, target, TENSOR, 0, (id(full), i))
                else:
                    held = r.rowsum[slot][s + 1]
                    self.release((id(held), i))
                    held[:, c] = total
                    copies[i] = self.send(
                        held.at[:, c], r.rowx[k][s].at[:, c], TENSOR, s + 1, (id(held), i)
                    )
            yield
        for copy in copies:
            copy.wait_recv()

    def scatter(self, buffer, landings, bits, finish):
        count, low = buffer.shape[0], 0
        for (axis, bit), landing in zip(bits, landings, strict=True):
            count //= 2
            mine = self.bit(axis, bit)
            keep = pl.multiple_of(low + mine * count, 8)
            give = pl.multiple_of(low + (1 - mine) * count, 8)
            copy = self.send(buffer.at[pl.ds(give, count)], landing, axis, bit)
            yield
            copy.wait_recv()
            buffer[pl.ds(keep, count), :] += landing[...]
            low = keep
        finish(buffer[pl.ds(low, count), :])

    def butterfly(self, held, landings, bits):
        for s, (axis, bit) in enumerate(bits):
            copy = self.send(held[s], landings[s], axis, bit)
            yield
            copy.wait_recv()
            held[s + 1][...] = held[s][...] + landings[s][...]


def drive(task):
    for _ in task:
        pass


def step(*tasks):
    for task in tasks:
        next(task, None)


def fused_kernel(z, *refs):
    ins, outs = len(Inputs._fields), len(Outputs._fields)
    r = SimpleNamespace(
        **Inputs(*refs[:ins])._asdict(),
        **Outputs(*refs[ins : ins + outs])._asdict(),
        **Scratch(*refs[ins + outs :])._asdict(),
    )
    flow = Flow(z, r)
    rows, width, channels, both, heads = z.rows, z.width, z.channels, z.both, z.heads
    inner = channels * z.tensor
    bf16, f32 = jnp.bfloat16, jnp.float32
    dp_at, tensor_at = flow.at[DP], flow.at[TENSOR]
    parity = flow.bit(DP, 0)
    my_rows = flow.half(flow.bit(TENSOR, 0))
    last = LAYERS - 1

    flow.barrier()

    def order(first):
        return [b for b in range(z.dp_bits) if b != first]

    def picker(first, side):
        low = [
            sum(((q >> (z.dp_bits - 2 - i)) & 1) << b for i, b in enumerate(order(first)))
            for q in range(z.blocks)
        ]
        bases = [owner * z.own for owner in low]
        return selection(width, bases, z.own, z.ownp, side * (z.own << first)).astype(bf16)

    far = min(1, z.dp_bits - 1)
    far_side = flow.bit(DP, far)
    far_mine, far_other = picker(far, far_side), picker(far, 1 - far_side)
    pick_mine, pick_other = picker(0, parity), picker(0, 1 - parity)
    shared_bases = [
        reversed_bits(p, z.dp_bits) * z.own + reversed_bits(t, z.tensor_bits) * z.cut
        for t in range(z.tensor)
        for p in range(z.dp)
    ]

    def pick_shared(t):
        group = shared_bases[t * z.dp : (t + 1) * z.dp]
        return selection(width, group, z.cut, z.cutp, 0).astype(bf16)

    cot_task = flow.shared_factor(
        r.to_db, r.from_db[last], matmul(r.cotangent[my_rows, :], far_other), far
    )
    step(cot_task)
    full = [r.full[0], r.output, r.full[1], r.input_grad]

    for l in range(LAYERS):
        given = [r.w_dt[head].astype(f32)[l : l + 1, :] for head in range(heads)]
        given.append(jnp.zeros((LANES - heads, width), f32))
        r.wdt[l] = jnp.concatenate(given, axis=0).astype(bf16)
        r.hvec[l] = jnp.zeros((8, LANES), f32)
        r.hvec[l, 0:1, :heads] = r.a_log[l : l + 1, :]
        r.hvec[l, 1:2, :heads] = r.d_skip[l : l + 1, :]
        r.hvec[l, 2:3, :heads] = r.dt_bias[l : l + 1, :]

    causal = triangle(rows)
    lower = jnp.where(causal, 1.0, 0.0)
    spread = head_map(channels)
    ones = jnp.ones((8, width), f32)
    eye = jnp.where(
        lax.broadcasted_iota(jnp.int32, (rows, rows), 0)
        == lax.broadcasted_iota(jnp.int32, (rows, rows), 1),
        1.0,
        0.0,
    )
    stat_row = lax.broadcasted_iota(jnp.int32, (8, rows), 0)
    factors = {}

    def column(stat):
        return exact(eye, stat, COLS_COLS)

    def residual(l):
        return r.tokens[...].astype(f32) if l == 0 else r.resid[l - 1]

    def forward(l):
        h = residual(l)
        scale = lax.rsqrt(jnp.mean(h * h, axis=1, keepdims=True) + EPSILON)
        normed = (h * scale * r.norm_gain[l : l + 1, :]).astype(bf16)
        r.normed[l] = normed
        normed_task = flow.shared_factor(
            r.to_normed, r.from_normed[l], matmul(r.normed[l, my_rows, :], pick_other), 0
        )
        step(normed_task)
        zg = matmul(normed, r.w_z[l])
        xi = matmul(normed, r.w_x[l])
        bci = matmul(normed, r.w_bc[l])
        dti = matmul(normed, r.wdt[l], COLS_COLS)
        r.zg[l] = zg
        r.xi[l] = xi
        r.bci[l] = bci
        r.dti[l] = dti
        hvec = r.hvec[l]
        pre_x = causal_conv(xi, r.conv_x[l], r.conv_x_bias[l : l + 1, :])
        xc = pre_x * sigmoid(pre_x)
        pre_b = causal_conv(bci, r.conv_bc[l], r.conv_bc_bias[l : l + 1, :])
        bcc = pre_b * sigmoid(pre_b)
        state = both // 2
        dt = softplus(dti + hvec[2:3, :])
        rate = -jnp.exp(hvec[0:1, :]) * dt
        log_decay = exact(lower, rate)
        log_decay_t = exact(rate, lower, ((0,), (1,)))
        xdt = (xc * exact(dt, spread, COLS_COLS)).astype(SCAN)
        scores = scan_dot(bcc[:, state:].astype(SCAN), bcc[:, :state].astype(SCAN), COLS_COLS)
        for head in range(heads):
            cols = slice(head * P_SIZE, (head + 1) * P_SIZE)
            weights = scores * decay_of(log_decay, log_decay_t, head, causal)
            r.y[l, :, cols] = scan_dot(weights.astype(SCAN), xdt[:, cols])
        y = r.y[l] + exact(hvec, spread, COLS_COLS)[1:2, :] * xc
        core = y * (zg * sigmoid(zg))
        gated = (core * r.gate_gain[l : l + 1, :]).astype(bf16)
        partial = matmul(gated, r.w_out[l])
        sum_task = flow.row_sum(l, partial, full[l])
        step(sum_task)
        stat = jnp.where(stat_row == 0, exact(ones[:, :channels], core * core, COLS_COLS), 0.0)
        if l == last:
            product = exact(ones, r.cotangent[...].astype(f32) * partial, COLS_COLS)
            stat = jnp.where(stat_row == 1, product, stat)
        r.stat[l][0][...] = stat
        stat_task = flow.butterfly(r.stat[l], r.statin[l], flow.every(TENSOR))
        step(stat_task)
        r.gated[l] = gated
        copy = flow.factor(r.to_gated, r.from_gated[l], gated.astype(f32), far)
        if l < last:
            step(sum_task)
        step(stat_task)
        r.normed_sel[l] = matmul(normed, pick_mine).astype(bf16)
        drive(stat_task)
        stat = column(r.stat[l][z.tensor_bits][...])
        factors[l] = (lax.rsqrt(stat[:, 0:1] / inner + EPSILON), stat[:, 1:2])
        return sum_task, normed_task, copy

    gated_copies, normed_tasks = {}, {}
    for l in range(LAYERS):
        sum_task, normed_tasks[l], gated_copies[l] = forward(l)
        if l < last:
            step(cot_task, normed_tasks[l])
            drive(sum_task)
            r.resid[l] = residual(l) + factors[l][0] * full[l][...]

    output_task = sum_task
    statistic = flow.send(r.stat[last][z.tensor_bits], r.statin[last][z.tensor_bits], DP, far)
    sums = {"o": (r.sum_wout, r.in_wout), "z": (r.sum_wz, r.in_wz), "x": (r.sum_wx, r.in_wx)}
    owned = {"o": r.g_wout, "z": r.g_wz, "x": r.g_wx, "b": r.g_wbc}
    tasks = {}

    def finish_to(m, l, count):
        def finish(value):
            owned[m][l] = value[:count, :]

        return finish

    def start_scatter(m, l, value):
        total, landings = sums[m]
        total[l][...] = value
        bits = [(DP, b) for b in order(far if m == "o" else 0)]
        tasks[m, l] = flow.scatter(total[l], landings[l], bits, finish_to(m, l, z.own))
        step(tasks[m, l])

    def weight_product(m, l, copy):
        sent, landing = {"z": (r.to_dzg, r.from_dzg), "x": (r.to_dxi, r.from_dxi)}[m]
        own = matmul(r.normed_sel[l], sent[...].astype(bf16), ROWS_ROWS)
        copy.wait_recv()
        theirs = matmul(
            r.from_normed[l][...].astype(bf16), landing[l][...].astype(bf16), ROWS_ROWS
        )
        start_scatter(m, l, own + theirs)

    def wout_product(l, db, their_db):
        own = matmul(matmul(db, far_mine).astype(bf16), r.gated[l], ROWS_ROWS)
        theirs = matmul(their_db, r.from_gated[l][...].astype(bf16), ROWS_ROWS)
        start_scatter("o", l, own + theirs)

    def small_task(l):
        yield from flow.butterfly(r.small[l], r.smallin[l], flow.every(DP))
        small = r.small[l][z.dp_bits][...]
        r.bcc[l][0][...] = small[0:8, width - both :]
        pick = selection(width, [0], z.own, z.own, dp_at * z.own)
        r.g_norm[l : l + 1, :] = exact(small[0:8, :], pick)[6:7, :]
        by_head = exact(small[8:, :], pick)
        for head in range(heads):
            r.g_wdt[head, l : l + 1, :] = by_head[head : head + 1, :]
            pick = selection(channels, [0], z.lanes, z.lanes, head * P_SIZE + dp_at * z.lanes)
            chan = exact(small[0:8, :channels], pick)
            for row in range(K + 2):
                r.g_chan[row, head, l : l + 1, :] = chan[row : row + 1, :]
        for row in range(3):
            r.g_heads[row, l : l + 1, :] = small[row : row + 1, channels : channels + heads]
        yield from flow.butterfly(r.bcc[l], r.bccin[l], flow.every(TENSOR))
        pick = selection(both, [0], z.piece, z.piece, (dp_at * z.tensor + tensor_at) * z.piece)
        bcc = exact(r.bcc[l][z.tensor_bits][...], pick)
        for row in range(K + 1):
            r.g_bcc[row, l : l + 1, :] = bcc[row : row + 1, :]

    copies = {}

    def backward(l, g):
        f, product = factors[l]
        normed = r.normed[l]
        db = (g * f).astype(bf16)
        if l != last:
            r.db_all[...] = db
            db_task = flow.shared_factor(
                r.to_db, r.from_db[l], matmul(r.db_all[my_rows, :], far_other), far
            )
            step(db_task)
            product = jnp.sum(g * full[l][...], axis=1, keepdims=True)
        small = r.small[l][0]
        small[...] = jnp.zeros_like(small)
        zg = r.zg[l]
        xi = r.xi[l]
        hvec = r.hvec[l]
        skip = exact(hvec, spread, COLS_COLS)[1:2, :]
        taps_x = r.conv_x[l]
        taps_b = r.conv_bc[l]
        pre_x = causal_conv(xi, taps_x, r.conv_x_bias[l : l + 1, :])
        sx = sigmoid(pre_x)
        xc = pre_x * sx
        within = r.y[l]
        y = within + skip * xc
        gate = r.gate_gain[l : l + 1, :]
        sz = sigmoid(zg)
        silu = zg * sz
        core = y * silu
        dgated = matmul(db, r.w_out[l], COLS_COLS)
        dms = -0.5 * f * f * f * product
        dcore = dgated * gate + dms * (2.0 / inner) * core
        dy = dcore * silu
        dzg = (dcore * y * (sz * (1.0 + zg * (1.0 - sz)))).astype(bf16)
        copies["z", l] = flow.factor(r.to_dzg, r.from_dzg[l], dzg.astype(f32), 0)
        back = matmul(dzg, r.w_z[l], COLS_COLS)

        if l == last:
            step(output_task)
            step(normed_tasks[last])
            drive(cot_task)
            drive(normed_tasks[0])
        else:
            weight_product("x", last, copies["x", last])

        bci = r.bci[l]
        dti = r.dti[l]
        pre_b = causal_conv(bci, taps_b, r.conv_bc_bias[l : l + 1, :])
        sb = sigmoid(pre_b)
        bcc = pre_b * sb
        state = both // 2
        keys = bcc[:, :state].astype(SCAN)
        queries = bcc[:, state:].astype(SCAN)
        raw = dti + hvec[2:3, :]
        dt = softplus(raw)
        neg = -jnp.exp(hvec[0:1, :])
        rate = neg * dt
        log_decay = exact(lower, rate)
        log_decay_t = exact(rate, lower, ((0,), (1,)))
        dt_full = exact(dt, spread, COLS_COLS)
        xdt = (xc * dt_full).astype(SCAN)
        dys = dy.astype(SCAN)
        scores = scan_dot(queries, keys, COLS_COLS)
        dscores = jnp.zeros_like(scores)
        for head in range(heads):
            cols = slice(head * P_SIZE, (head + 1) * P_SIZE)
            decay = decay_of(log_decay, log_decay_t, head, causal)
            dy_h = dys[:, cols]
            dscores = dscores + scan_dot(dy_h, xdt[:, cols], COLS_COLS) * decay
            r.dxdt[:, cols] = scan_dot((scores * decay).astype(SCAN), dy_h, ROWS_ROWS)
        dxdt = r.dxdt[...]

        dpre_x = (dxdt * dt_full + skip * dy) * (sx * (1.0 + pre_x * (1.0 - sx)))
        dxi = conv_back(taps_x, dpre_x).astype(bf16)
        copies["x", l] = flow.factor(r.to_dxi, r.from_dxi[l], dxi.astype(f32), 0)
        back = back + matmul(dxi, r.w_x[l], COLS_COLS)

        if l == last:
            drive(normed_tasks[last])
            gated_copies[0].wait_recv()
            gated_copies[last].wait_recv()
            statistic.wait_recv()
            stat = column(r.statin[last][z.tensor_bits][...])
            their_f = lax.rsqrt(stat[:, 0:1] / inner + EPSILON)
            wout_product(l, db, (r.from_db[l][...] * their_f).astype(bf16))
        else:
            step(db_task)

        dlog = exact(dys.astype(f32) * within - xdt.astype(f32) * dxdt, spread)
        drate = exact(lower, dlog, ROWS_ROWS)
        ddt = exact(dxdt * xc, spread) + drate * neg
        draw = ddt * sigmoid(raw)
        ddti = draw.astype(bf16)
        back = back + matmul(ddti, r.wdt[l])

        dscores = dscores.astype(SCAN)
        dkeys = scan_dot(dscores, queries, ROWS_ROWS)
        dqueries = scan_dot(dscores, keys)
        dbcc = jnp.concatenate([dkeys, dqueries], axis=1)
        dpre_b = dbcc * (sb * (1.0 + pre_b * (1.0 - sb)))
        dbci = conv_back(taps_b, dpre_b).astype(bf16)
        k = 2 * LAYERS - 1 - l
        back = back + matmul(dbci, r.w_bc[l], COLS_COLS)
        back_task = flow.row_sum(k, back, full[k])
        step(back_task)
        if l == last:
            step(output_task)
        step(back_task)
        for t in range(z.tensor):
            picked = matmul(normed, pick_shared(t)).astype(bf16)
            group = z.dp * z.cutp
            r.sum_wbc[l][t * group : (t + 1) * group, :] = matmul(picked, dbci, ROWS_ROWS)

        bits = flow.every(TENSOR) + flow.every(DP)
        tasks["b", l] = flow.scatter(
            r.sum_wbc[l], r.in_wbc[l], bits, finish_to("b", l, z.cut)
        )
        step(tasks["b", l])
        sides = (
            (slice(0, channels), r.xi[l], dpre_x),
            (slice(width - both, width), r.bci[l], dpre_b),
        )
        for at, signal, back_pre in sides:
            for tap in range(K):
                small[tap : tap + 1, at] = jnp.sum(
                    back_pre * delayed(signal, K - 1 - tap), axis=0, keepdims=True
                )
            small[K : K + 1, at] = jnp.sum(back_pre, axis=0, keepdims=True)
        small[K + 1 : K + 2, :channels] = jnp.sum(dgated * core, axis=0, keepdims=True)
        at = slice(channels, channels + LANES)
        small[0:1, at] = jnp.sum(drate * rate, axis=0, keepdims=True)
        small[1:2, at] = exact(jnp.sum(dy * xc, axis=0, keepdims=True) + jnp.zeros((8, 1), f32), spread)[0:1, :]
        small[2:3, at] = jnp.sum(draw, axis=0, keepdims=True)
        small[8:, :] = matmul(ddti, normed, ROWS_ROWS)[: z.head_rows, :]
        if l == last:
            weight_product("z", l, copies["z", l])
            drive(output_task)
            for i in range(CHUNKS):
                flow.release((id(r.output), i))
            r.output[...] = residual(l) + f * r.output[...]
        else:
            step(tasks["o", last])
            step(tasks["z", last])
            drive(db_task)
            wout_product(l, db, r.from_db[l][...].astype(bf16))
            weight_product("z", l, copies["z", l])
            step(tasks["b", last])
            step(tasks["s", last])
            step(tasks["x", last])
            step(tasks["o", last])
        step(tasks["b", l])
        drive(back_task)

        h = residual(l)
        back_normed = full[k][...]
        scale = lax.rsqrt(jnp.mean(h * h, axis=1, keepdims=True) + EPSILON)
        small[6:7, :] = jnp.sum(back_normed * h * scale, axis=0, keepdims=True)
        tasks["s", l] = small_task(l)
        step(tasks["s", l])
        hat = back_normed * r.norm_gain[l : l + 1, :]
        return g + scale * hat - scale * scale * scale * h * jnp.mean(
            hat * h, axis=1, keepdims=True
        )

    g = r.cotangent[...].astype(f32)
    for l in reversed(range(LAYERS)):
        g = backward(l, g)
    for i in range(CHUNKS):
        flow.release((id(r.input_grad), i))
    r.input_grad[...] = g
    weight_product("x", 0, copies["x", 0])
    pending = [tasks[m, l] for m, l in TAIL]
    while pending:
        left = []
        for task in pending:
            if next(task, pending) is not pending:
                left.append(task)
        pending = left
    flow.drain()


TAIL = (("z", 0), ("s", 0), ("x", 0), ("o", 0), ("b", 0)) + tuple((m, LAYERS - 1) for m in "xzosb")


def deliver_kernel(count, *refs):
    for i in range(count):
        refs[count + i][...] = refs[i][...]


def on_device(dp_size, tensor_size, *args):
    given = Inputs(*args)
    rows, width = given.tokens.shape
    z = Sizes(
        dp_size,
        tensor_size,
        rows,
        width,
        given.w_z.shape[2],
        given.w_bc.shape[2],
        given.w_dt.shape[2],
    )
    given = given._replace(w_dt=jnp.transpose(given.w_dt, (2, 0, 1)))
    outs = out_shapes(z)
    results = pl.pallas_call(
        functools.partial(fused_kernel, z),
        out_shape=outs,
        in_specs=[pl.BlockSpec(memory_space=pltpu.VMEM)] * len(args),
        out_specs=[pl.BlockSpec(memory_space=pltpu.VMEM)] * len(outs),
        scratch_shapes=list(scratch_shapes(z)),
        compiler_params=pltpu.CompilerParams(
            collective_id=0, has_side_effects=True, vmem_limit_bytes=63 * 1024 * 1024
        ),
    )(*given)
    results = pl.pallas_call(
        functools.partial(deliver_kernel, len(outs)),
        out_shape=outs,
        in_specs=[pl.BlockSpec(memory_space=pltpu.VMEM)] * len(outs),
        out_specs=[pl.BlockSpec(memory_space=pltpu.VMEM)] * len(outs),
    )(*results)
    done = Outputs(*results)
    return tuple(
        done._replace(
            g_wdt=jnp.transpose(done.g_wdt, (1, 2, 0)),
            g_wout=jnp.swapaxes(done.g_wout, 1, 2),
            g_chan=jnp.transpose(done.g_chan, (2, 0, 1, 3)),
            g_bcc=jnp.swapaxes(done.g_bcc, 0, 1),
            g_heads=jnp.swapaxes(done.g_heads, 0, 1),
        )
    )


def solution(mesh):
    placed = (
        P(DP, None),
        P(DP, None),
        P(),
        P(None, None, TENSOR),
        P(None, None, TENSOR),
        P(),
        P(None, None, TENSOR),
        P(None, None, TENSOR),
        P(None, TENSOR),
        P(),
        P(),
        P(None, TENSOR),
        P(None, TENSOR),
        P(None, TENSOR),
        P(None, TENSOR),
        P(None, TENSOR, None),
    )
    return jax.shard_map(
        functools.partial(on_device, mesh.shape[DP], mesh.shape[TENSOR]),
        mesh=mesh,
        in_specs=placed,
        out_specs=(
            P(DP, None),
            P(DP, None),
            P(None, DP),
            P(None, DP, TENSOR),
            P(None, DP, TENSOR),
            P(None, DP, TENSOR),
            P(None, TENSOR, DP),
            P(None, None, TENSOR, DP),
            P(None, (DP, TENSOR), None),
            P(None, None, (DP, TENSOR)),
            P(None, None, TENSOR),
        ),
        check_vma=False,
    )
```

```python
import functools
from types import SimpleNamespace
from typing import Any, NamedTuple

import jax
import jax.numpy as jnp
from jax import lax
from jax.experimental import pallas as pl
from jax.experimental.pallas import tpu as pltpu
from jax.sharding import PartitionSpec as P

P_SIZE = 64
K = 4
LANES = 128
DP, TENSOR = "dp", "tensor"
LENGTH = 256
LAYERS = 2
EPSILON = 1e-05
HIGHEST_PREC = lax.Precision.HIGHEST
MESH = pl.DeviceIdType.MESH
ROWS_ROWS = ((0,), (0,))
COLS_COLS = ((1,), (1,))


def matmul(left, right, dims=((1,), (0,)), precision=None):
    return lax.dot_general(
        left, right, (dims, ((), ())), precision=precision, preferred_element_type=jnp.float32
    )


def exact(left, right, dims=((1,), (0,))):
    return matmul(left, right, dims, HIGHEST_PREC)


def sigmoid(value):
    return 1.0 / (1.0 + jnp.exp(-value))


def softplus(value):
    return jnp.maximum(value, 0.0) + jnp.log1p(jnp.exp(-jnp.abs(value)))


def delayed(signal, shift):
    if shift == 0:
        return signal
    rows = signal.shape[0]
    moved = pltpu.roll(signal, shift % rows, 0)
    at = lax.broadcasted_iota(jnp.int32, signal.shape, 0)
    inside = at >= shift if shift > 0 else at < rows + shift
    return jnp.where(inside, moved, 0.0)


def causal_conv(signal, taps, offset):
    total = offset
    for k in range(K):
        total = total + taps[k : k + 1, :] * delayed(signal, K - 1 - k)
    return total


def conv_back(taps, back):
    total = jnp.zeros_like(back)
    for k in range(K):
        total = total + taps[k : k + 1, :] * delayed(back, k + 1 - K)
    return total


def triangle(rows):
    down = lax.broadcasted_iota(jnp.int32, (rows, rows), 0)
    across = lax.broadcasted_iota(jnp.int32, (rows, rows), 1)
    return down >= across


def head_map(channels):
    channel = lax.broadcasted_iota(jnp.int32, (channels, LANES), 0)
    head = lax.broadcasted_iota(jnp.int32, (channels, LANES), 1)
    return jnp.where(channel // P_SIZE == head, 1.0, 0.0)


def decay_of(log_decay, log_decay_t, head, causal):
    gap = log_decay[:, head : head + 1] - log_decay_t[head : head + 1, :]
    return jnp.where(causal, jnp.exp(jnp.where(causal, gap, 0.0)), 0.0)


def up8(count):
    return -(-count // 8) * 8


def bits_of(size):
    return size.bit_length() - 1


def reversed_bits(value, count):
    return sum(((value >> i) & 1) << (count - 1 - i) for i in range(count))


def selection(width, bases, keep, step, shift):
    columns = len(bases) * step
    at = lax.broadcasted_iota(jnp.int32, (1, columns), 1)
    feature = at + bases[0]
    part = at
    for q in range(1, len(bases)):
        move = bases[q] - bases[q - 1] - step
        inside = at >= q * step
        feature = feature + jnp.where(inside, move, 0)
        part = part - jnp.where(inside, step, 0)
    feature = feature + shift
    if keep != step:
        feature = jnp.where(part < keep, feature, -1)
    row = lax.broadcasted_iota(jnp.int32, (width, columns), 0)
    return jnp.where(row == feature, 1.0, 0.0)


class Sizes:
    def __init__(self, dp, tensor, rows, width, channels, both, heads):
        self.dp, self.tensor = dp, tensor
        self.rows, self.width, self.channels = rows, width, channels
        self.both, self.heads = both, heads
        self.dp_bits, self.tensor_bits = bits_of(dp), bits_of(tensor)
        assert dp == 1 << self.dp_bits and tensor == 1 << self.tensor_bits
        assert self.dp_bits >= 1 and self.tensor_bits >= 1 and rows == LENGTH
        self.own = width // dp
        self.ownp = up8(self.own)
        self.blocks = dp // 2
        self.half = self.blocks * self.ownp
        self.cut = self.own // tensor
        self.cutp = up8(self.cut)
        self.shared = dp * tensor * self.cutp
        self.lanes = P_SIZE // dp
        self.piece = both // (dp * tensor)
        self.head_rows = up8(heads)
        self.small = 8 + self.head_rows


class Inputs(NamedTuple):
    tokens: Any
    cotangent: Any
    norm_gain: Any
    w_z: Any
    w_x: Any
    w_bc: Any
    w_dt: Any
    conv_x: Any
    conv_x_bias: Any
    conv_bc: Any
    conv_bc_bias: Any
    dt_bias: Any
    a_log: Any
    d_skip: Any
    gate_gain: Any
    w_out: Any


class Outputs(NamedTuple):
    output: Any
    input_grad: Any
    g_norm: Any
    g_wz: Any
    g_wx: Any
    g_wdt: Any
    g_wout: Any
    g_chan: Any
    g_wbc: Any
    g_bcc: Any
    g_heads: Any


def out_shapes(z):
    shapes = Outputs(
        output=(z.rows, z.width),
        input_grad=(z.rows, z.width),
        g_norm=(LAYERS, z.own),
        g_wz=(LAYERS, z.own, z.channels),
        g_wx=(LAYERS, z.own, z.channels),
        g_wdt=(z.heads, LAYERS, z.own),
        g_wout=(LAYERS, z.own, z.channels),
        g_chan=(K + 2, z.heads, LAYERS, z.lanes),
        g_wbc=(LAYERS, z.cut, z.both),
        g_bcc=(K + 1, LAYERS, z.piece),
        g_heads=(3, LAYERS, z.heads),
    )
    return [jax.ShapeDtypeStruct(shape, jnp.float32) for shape in shapes]


def scratch_shapes(z):
    f32, bf16 = jnp.float32, jnp.bfloat16
    rows, width, channels, both = z.rows, z.width, z.channels, z.both

    def new(*shape):
        return pltpu.VMEM(shape, f32)

    def steps(count, *shape):
        return [new(*shape) for _ in range(count)]

    def layers(make):
        return [make() for _ in range(LAYERS)]

    def halves(start, first, count, columns):
        return [new(start >> s, columns) for s in range(first, count)]

    per_sum = range(2 * LAYERS)
    return Scratch(
            wdt=pltpu.VMEM((LAYERS, LANES, width), bf16),
            hvec=new(LAYERS, 8, LANES),
            resid=new(LAYERS - 1, rows, width),
            normed=pltpu.VMEM((LAYERS, rows, width), bf16),
            zg=new(LAYERS, rows, channels),
            xi=new(LAYERS, rows, channels),
            bci=new(LAYERS, rows, both),
            dti=new(LAYERS, rows, LANES),
            y=new(LAYERS, rows, channels),
            dxdt=new(rows, channels),
            part=steps(2, rows, width),
            rowsum=[steps(z.tensor_bits, rows // 2, width) for _ in range(2)],
            rowin=steps(2 * LAYERS, rows // 2, width),
            rowx=[steps(z.tensor_bits, rows // 2, width)[1:] for _ in per_sum],
            full=steps(2, rows, width),
            stat=layers(lambda: steps(z.tensor_bits + 1, 8, rows)),
            statin=layers(lambda: steps(z.tensor_bits + 1, 8, rows)),
            to_normed=new(rows // 2, z.half),
            to_db=new(rows // 2, z.half),
            db_all=pltpu.VMEM((rows, width), bf16),
            to_gated=new(rows, channels),
            to_dzg=new(rows, channels),
            to_dxi=new(rows, channels),
            from_normed=steps(LAYERS, rows, z.half),
            from_db=steps(LAYERS, rows, z.half),
            from_gated=steps(LAYERS, rows, channels),
            from_dzg=steps(LAYERS, rows, channels),
            from_dxi=steps(LAYERS, rows, channels),
            normed_sel=pltpu.VMEM((LAYERS, rows, z.half), bf16),
            gated=pltpu.VMEM((LAYERS, rows, channels), bf16),
            sum_wout=steps(LAYERS, z.half, channels),
            sum_wz=steps(LAYERS, z.half, channels),
            sum_wx=steps(LAYERS, z.half, channels),
            in_wout=layers(lambda: halves(z.half, 1, z.dp_bits, channels)),
            in_wz=layers(lambda: halves(z.half, 1, z.dp_bits, channels)),
            in_wx=layers(lambda: halves(z.half, 1, z.dp_bits, channels)),
            sum_wbc=steps(LAYERS, z.shared, both),
            in_wbc=layers(lambda: halves(z.shared, 1, z.tensor_bits + z.dp_bits + 1, both)),
            small=layers(lambda: steps(z.dp_bits + 1, z.small, width)),
            smallin=layers(lambda: steps(z.dp_bits, z.small, width)),
            bcc=layers(lambda: steps(z.tensor_bits + 1, 8, both)),
            bccin=layers(lambda: steps(z.tensor_bits, 8, both)),
            send_sem=pltpu.SemaphoreType.DMA((COPIES,)),
            recv_sem=pltpu.SemaphoreType.DMA((COPIES,)),
    )


class Scratch(NamedTuple):
    wdt: Any
    hvec: Any
    resid: Any
    normed: Any
    zg: Any
    xi: Any
    bci: Any
    dti: Any
    y: Any
    dxdt: Any
    part: Any
    rowsum: Any
    rowin: Any
    rowx: Any
    full: Any
    stat: Any
    statin: Any
    to_normed: Any
    to_db: Any
    db_all: Any
    to_gated: Any
    to_dzg: Any
    to_dxi: Any
    from_normed: Any
    from_db: Any
    from_gated: Any
    from_dzg: Any
    from_dxi: Any
    normed_sel: Any
    gated: Any
    sum_wout: Any
    sum_wz: Any
    sum_wx: Any
    in_wout: Any
    in_wz: Any
    in_wx: Any
    sum_wbc: Any
    in_wbc: Any
    small: Any
    smallin: Any
    bcc: Any
    bccin: Any
    send_sem: Any
    recv_sem: Any


COPIES = 160
CHUNKS = 2
SCAN = jnp.bfloat16


def scan_dot(left, right, dims=((1,), (0,))):
    return matmul(left, right, dims, HIGHEST_PREC if SCAN == jnp.float32 else None)


class Flow:
    def __init__(self, z, r):
        self.z, self.r = z, r
        self.at = {DP: lax.axis_index(DP), TENSOR: lax.axis_index(TENSOR)}
        self.copies = []
        self.leaving = {}
        self.done = set()

    def bit(self, axis, bit):
        return lax.rem(lax.div(self.at[axis], 1 << bit), 2)

    def peer(self, axis, bit):
        there = dict(self.at)
        there[axis] = self.at[axis] + (1 << bit) * (1 - 2 * self.bit(axis, bit))
        return (there[DP], there[TENSOR])

    def every(self, axis):
        count = self.z.dp_bits if axis == DP else self.z.tensor_bits
        return [(axis, b) for b in range(count)]

    def barrier(self):
        everyone = self.every(DP) + self.every(TENSOR)
        barrier = pltpu.get_barrier_semaphore()
        for axis, bit in everyone:
            pl.semaphore_signal(
                barrier, inc=1, device_id=self.peer(axis, bit), device_id_type=MESH
            )
        pl.semaphore_wait(barrier, len(everyone))

    def release(self, key):
        index = self.leaving.pop(key, None)
        if index is not None:
            self.copies[index].wait_send()
            self.done.add(index)

    def send(self, source, target, axis, bit, key=None):
        index = len(self.copies)
        if key is not None:
            self.leaving[key] = index
        copy = pltpu.make_async_remote_copy(
            src_ref=source,
            dst_ref=target,
            send_sem=self.r.send_sem.at[index],
            recv_sem=self.r.recv_sem.at[index],
            device_id=self.peer(axis, bit),
            device_id_type=MESH,
        )
        copy.start()
        self.copies.append(copy)
        return copy

    def drain(self):
        for index, copy in enumerate(self.copies):
            if index not in self.done:
                copy.wait_send()

    def half(self, which):
        count = self.z.rows // 2
        return pl.ds(pl.multiple_of(which * count, 16), count)

    def factor(self, source, landing, value, bit):
        self.release(id(source))
        source[...] = value
        return self.send(source, landing, DP, bit, id(source))

    def shared_factor(self, source, landing, value, bit):
        mine = self.half(self.bit(TENSOR, 0))
        self.release(id(source))
        source[...] = value
        copy = self.send(source, landing.at[mine], DP, bit, id(source))
        yield
        copy.wait_recv()
        copy = self.send(landing.at[mine], landing.at[mine], TENSOR, 0)
        yield
        copy.wait_recv()

    def row_sum(self, k, value, full):
        r = self.r
        bit = self.bit(TENSOR, 0)
        here, there = self.half(bit), self.half(1 - bit)
        slot = k % 2
        part = r.part[slot]
        width = part.shape[1] // CHUNKS
        chunks = [pl.ds(i * width, width) for i in range(CHUNKS)]
        for i in range(CHUNKS):
            self.release((id(part), i))
        part[...] = value
        copies = [
            self.send(part.at[there, c], r.rowin[k].at[:, c], TENSOR, 0, (id(part), i))
            for i, c in enumerate(chunks)
        ]
        yield
        for s in range(self.z.tensor_bits):
            for i, c in enumerate(chunks):
                copies[i].wait_recv()
                if s == 0:
                    total = part[here, c] + r.rowin[k][:, c]
                else:
                    total = r.rowsum[slot][s][:, c] + r.rowx[k][s - 1][:, c]
                if s == self.z.tensor_bits - 1:
                    full[here, c] = total
                    target = full.at[here, c]
                    copies[i] = self.send(target, target, TENSOR, 0, (id(full), i))
                else:
                    held = r.rowsum[slot][s + 1]
                    self.release((id(held), i))
                    held[:, c] = total
                    copies[i] = self.send(
                        held.at[:, c], r.rowx[k][s].at[:, c], TENSOR, s + 1, (id(held), i)
                    )
            yield
        for copy in copies:
            copy.wait_recv()

    def scatter(self, buffer, landings, bits, finish):
        count, low = buffer.shape[0], 0
        for (axis, bit), landing in zip(bits, landings, strict=True):
            count //= 2
            mine = self.bit(axis, bit)
            keep = pl.multiple_of(low + mine * count, 8)
            give = pl.multiple_of(low + (1 - mine) * count, 8)
            copy = self.send(buffer.at[pl.ds(give, count)], landing, axis, bit)
            yield
            copy.wait_recv()
            buffer[pl.ds(keep, count), :] += landing[...]
            low = keep
        finish(buffer[pl.ds(low, count), :])


    def butterfly(self, held, landings, bits):
        for s, (axis, bit) in enumerate(bits):
            copy = self.send(held[s], landings[s], axis, bit)
            yield
            copy.wait_recv()
            held[s + 1][...] = held[s][...] + landings[s][...]


def drive(task):
    for _ in task:
        pass


def step(*tasks):
    for task in tasks:
        next(task, None)


def fused_kernel(z, *refs):
    ins, outs = len(Inputs._fields), len(Outputs._fields)
    r = SimpleNamespace(
        **Inputs(*refs[:ins])._asdict(),
        **Outputs(*refs[ins : ins + outs])._asdict(),
        **Scratch(*refs[ins + outs :])._asdict(),
    )
    flow = Flow(z, r)
    rows, width, channels, both, heads = z.rows, z.width, z.channels, z.both, z.heads
    inner = channels * z.tensor
    bf16, f32 = jnp.bfloat16, jnp.float32
    dp_at, tensor_at = flow.at[DP], flow.at[TENSOR]
    parity = flow.bit(DP, 0)
    my_rows = flow.half(flow.bit(TENSOR, 0))
    last = LAYERS - 1

    flow.barrier()

    def order(first):
        return [b for b in range(z.dp_bits) if b != first]

    def picker(first, side):
        low = [
            sum(((q >> (z.dp_bits - 2 - i)) & 1) << b for i, b in enumerate(order(first)))
            for q in range(z.blocks)
        ]
        bases = [owner * z.own for owner in low]
        return selection(width, bases, z.own, z.ownp, side * (z.own << first)).astype(bf16)

    far = min(1, z.dp_bits - 1)
    far_side = flow.bit(DP, far)
    far_mine, far_other = picker(far, far_side), picker(far, 1 - far_side)
    pick_mine, pick_other = picker(0, parity), picker(0, 1 - parity)
    shared_bases = [
        reversed_bits(p, z.dp_bits) * z.own + reversed_bits(t, z.tensor_bits) * z.cut
        for t in range(z.tensor)
        for p in range(z.dp)
    ]

    def pick_shared(t):
        group = shared_bases[t * z.dp : (t + 1) * z.dp]
        return selection(width, group, z.cut, z.cutp, 0).astype(bf16)

    cot_task = flow.shared_factor(
        r.to_db, r.from_db[last], matmul(r.cotangent[my_rows, :], far_other), far
    )
    step(cot_task)
    full = [r.full[0], r.output, r.full[1], r.input_grad]

    for l in range(LAYERS):
        given = [r.w_dt[head].astype(f32)[l : l + 1, :] for head in range(heads)]
        given.append(jnp.zeros((LANES - heads, width), f32))
        r.wdt[l] = jnp.concatenate(given, axis=0).astype(bf16)
        r.hvec[l] = jnp.zeros((8, LANES), f32)
        r.hvec[l, 0:1, :heads] = r.a_log[l : l + 1, :]
        r.hvec[l, 1:2, :heads] = r.d_skip[l : l + 1, :]
        r.hvec[l, 2:3, :heads] = r.dt_bias[l : l + 1, :]

    causal = triangle(rows)
    lower = jnp.where(causal, 1.0, 0.0)
    spread = head_map(channels)
    ones = jnp.ones((8, width), f32)
    eye = jnp.where(
        lax.broadcasted_iota(jnp.int32, (rows, rows), 0)
        == lax.broadcasted_iota(jnp.int32, (rows, rows), 1),
        1.0,
        0.0,
    )
    stat_row = lax.broadcasted_iota(jnp.int32, (8, rows), 0)
    factors = {}

    def column(stat):
        return exact(eye, stat, COLS_COLS)

    def residual(l):
        return r.tokens[...].astype(f32) if l == 0 else r.resid[l - 1]

    def forward(l):
        h = residual(l)
        scale = lax.rsqrt(jnp.mean(h * h, axis=1, keepdims=True) + EPSILON)
        normed = (h * scale * r.norm_gain[l : l + 1, :]).astype(bf16)
        r.normed[l] = normed
        normed_task = flow.shared_factor(
            r.to_normed, r.from_normed[l], matmul(r.normed[l, my_rows, :], pick_other), 0
        )
        step(normed_task)
        zg = matmul(normed, r.w_z[l])
        xi = matmul(normed, r.w_x[l])
        bci = matmul(normed, r.w_bc[l])
        dti = matmul(normed, r.wdt[l], COLS_COLS)
        r.zg[l] = zg
        r.xi[l] = xi
        r.bci[l] = bci
        r.dti[l] = dti
        hvec = r.hvec[l]
        pre_x = causal_conv(xi, r.conv_x[l], r.conv_x_bias[l : l + 1, :])
        xc = pre_x * sigmoid(pre_x)
        pre_b = causal_conv(bci, r.conv_bc[l], r.conv_bc_bias[l : l + 1, :])
        bcc = pre_b * sigmoid(pre_b)
        state = both // 2
        dt = softplus(dti + hvec[2:3, :])
        rate = -jnp.exp(hvec[0:1, :]) * dt
        log_decay = exact(lower, rate)
        log_decay_t = exact(rate, lower, ((0,), (1,)))
        xdt = (xc * exact(dt, spread, COLS_COLS)).astype(SCAN)
        scores = scan_dot(bcc[:, state:].astype(SCAN), bcc[:, :state].astype(SCAN), COLS_COLS)
        for head in range(heads):
            cols = slice(head * P_SIZE, (head + 1) * P_SIZE)
            weights = scores * decay_of(log_decay, log_decay_t, head, causal)
            r.y[l, :, cols] = scan_dot(weights.astype(SCAN), xdt[:, cols])
        y = r.y[l] + exact(hvec, spread, COLS_COLS)[1:2, :] * xc
        core = y * (zg * sigmoid(zg))
        gated = (core * r.gate_gain[l : l + 1, :]).astype(bf16)
        partial = matmul(gated, r.w_out[l])
        sum_task = flow.row_sum(l, partial, full[l])
        step(sum_task)
        stat = jnp.where(stat_row == 0, exact(ones[:, :channels], core * core, COLS_COLS), 0.0)
        if l == last:
            product = exact(ones, r.cotangent[...].astype(f32) * partial, COLS_COLS)
            stat = jnp.where(stat_row == 1, product, stat)
        r.stat[l][0][...] = stat
        stat_task = flow.butterfly(r.stat[l], r.statin[l], flow.every(TENSOR))
        step(stat_task)
        r.gated[l] = gated
        copy = flow.factor(r.to_gated, r.from_gated[l], gated.astype(f32), far)
        if l < last:
            step(sum_task)
        step(stat_task)
        r.normed_sel[l] = matmul(normed, pick_mine).astype(bf16)
        drive(stat_task)
        stat = column(r.stat[l][z.tensor_bits][...])
        factors[l] = (lax.rsqrt(stat[:, 0:1] / inner + EPSILON), stat[:, 1:2])
        return sum_task, normed_task, copy

    gated_copies, normed_tasks = {}, {}
    for l in range(LAYERS):
        sum_task, normed_tasks[l], gated_copies[l] = forward(l)
        if l < last:
            step(cot_task, normed_tasks[l])
            drive(sum_task)
            r.resid[l] = residual(l) + factors[l][0] * full[l][...]

    output_task = sum_task
    statistic = flow.send(r.stat[last][z.tensor_bits], r.statin[last][z.tensor_bits], DP, far)
    sums = {"o": (r.sum_wout, r.in_wout), "z": (r.sum_wz, r.in_wz), "x": (r.sum_wx, r.in_wx)}
    owned = {"o": r.g_wout, "z": r.g_wz, "x": r.g_wx, "b": r.g_wbc}
    tasks = {}

    def finish_to(m, l, count):
        def finish(value):
            owned[m][l] = value[:count, :]

        return finish

    def start_scatter(m, l, value):
        total, landings = sums[m]
        total[l][...] = value
        bits = [(DP, b) for b in order(far if m == "o" else 0)]
        tasks[m, l] = flow.scatter(total[l], landings[l], bits, finish_to(m, l, z.own))
        step(tasks[m, l])

    def weight_product(m, l, copy):
        sent, landing = {"z": (r.to_dzg, r.from_dzg), "x": (r.to_dxi, r.from_dxi)}[m]
        own = matmul(r.normed_sel[l], sent[...].astype(bf16), ROWS_ROWS)
        if l != last:
            step(tasks["o", last], tasks["z", last], tasks["x", last])
        copy.wait_recv()
        theirs = matmul(
            r.from_normed[l][...].astype(bf16), landing[l][...].astype(bf16), ROWS_ROWS
        )
        start_scatter(m, l, own + theirs)

    def wout_product(l, db, their_db):
        own = matmul(matmul(db, far_mine).astype(bf16), r.gated[l], ROWS_ROWS)
        theirs = matmul(their_db, r.from_gated[l][...].astype(bf16), ROWS_ROWS)
        start_scatter("o", l, own + theirs)

    def small_task(l):
        yield from flow.butterfly(r.small[l], r.smallin[l], flow.every(DP))
        small = r.small[l][z.dp_bits][...]
        r.bcc[l][0][...] = small[0:8, width - both :]
        pick = selection(width, [0], z.own, z.own, dp_at * z.own)
        r.g_norm[l : l + 1, :] = exact(small[0:8, :], pick)[6:7, :]
        by_head = exact(small[8:, :], pick)
        for head in range(heads):
            r.g_wdt[head, l : l + 1, :] = by_head[head : head + 1, :]
            pick = selection(channels, [0], z.lanes, z.lanes, head * P_SIZE + dp_at * z.lanes)
            chan = exact(small[0:8, :channels], pick)
            for row in range(K + 2):
                r.g_chan[row, head, l : l + 1, :] = chan[row : row + 1, :]
        for row in range(3):
            r.g_heads[row, l : l + 1, :] = small[row : row + 1, channels : channels + heads]
        yield from flow.butterfly(r.bcc[l], r.bccin[l], flow.every(TENSOR))
        pick = selection(both, [0], z.piece, z.piece, (dp_at * z.tensor + tensor_at) * z.piece)
        bcc = exact(r.bcc[l][z.tensor_bits][...], pick)
        for row in range(K + 1):
            r.g_bcc[row, l : l + 1, :] = bcc[row : row + 1, :]

    copies = {}

    def backward(l, g):
        f, product = factors[l]
        normed = r.normed[l]
        db = (g * f).astype(bf16)
        if l != last:
            r.db_all[...] = db
            db_task = flow.shared_factor(
                r.to_db, r.from_db[l], matmul(r.db_all[my_rows, :], far_other), far
            )
            step(db_task)
            product = jnp.sum(g * full[l][...], axis=1, keepdims=True)
        small = r.small[l][0]
        small[...] = jnp.zeros_like(small)
        zg = r.zg[l]
        xi = r.xi[l]
        hvec = r.hvec[l]
        skip = exact(hvec, spread, COLS_COLS)[1:2, :]
        taps_x = r.conv_x[l]
        taps_b = r.conv_bc[l]
        pre_x = causal_conv(xi, taps_x, r.conv_x_bias[l : l + 1, :])
        sx = sigmoid(pre_x)
        xc = pre_x * sx
        within = r.y[l]
        y = within + skip * xc
        gate = r.gate_gain[l : l + 1, :]
        sz = sigmoid(zg)
        silu = zg * sz
        core = y * silu
        dgated = matmul(db, r.w_out[l], COLS_COLS)
        dms = -0.5 * f * f * f * product
        dcore = dgated * gate + dms * (2.0 / inner) * core
        dy = dcore * silu
        dzg = (dcore * y * (sz * (1.0 + zg * (1.0 - sz)))).astype(bf16)
        copies["z", l] = flow.factor(r.to_dzg, r.from_dzg[l], dzg.astype(f32), 0)
        back = matmul(dzg, r.w_z[l], COLS_COLS)

        if l == last:
            step(output_task)
            step(normed_tasks[last])
            drive(cot_task)
            drive(normed_tasks[0])
        else:
            weight_product("x", last, copies["x", last])

        bci = r.bci[l]
        dti = r.dti[l]
        pre_b = causal_conv(bci, taps_b, r.conv_bc_bias[l : l + 1, :])
        sb = sigmoid(pre_b)
        bcc = pre_b * sb
        state = both // 2
        keys = bcc[:, :state].astype(SCAN)
        queries = bcc[:, state:].astype(SCAN)
        raw = dti + hvec[2:3, :]
        dt = softplus(raw)
        neg = -jnp.exp(hvec[0:1, :])
        rate = neg * dt
        log_decay = exact(lower, rate)
        log_decay_t = exact(rate, lower, ((0,), (1,)))
        dt_full = exact(dt, spread, COLS_COLS)
        xdt = (xc * dt_full).astype(SCAN)
        dys = dy.astype(SCAN)
        scores = scan_dot(queries, keys, COLS_COLS)
        dscores = jnp.zeros_like(scores)
        for head in range(heads):
            cols = slice(head * P_SIZE, (head + 1) * P_SIZE)
            decay = decay_of(log_decay, log_decay_t, head, causal)
            dy_h = dys[:, cols]
            dscores = dscores + scan_dot(dy_h, xdt[:, cols], COLS_COLS) * decay
            r.dxdt[:, cols] = scan_dot((scores * decay).astype(SCAN), dy_h, ROWS_ROWS)
        dxdt = r.dxdt[...]

        dpre_x = (dxdt * dt_full + skip * dy) * (sx * (1.0 + pre_x * (1.0 - sx)))
        dxi = conv_back(taps_x, dpre_x).astype(bf16)
        copies["x", l] = flow.factor(r.to_dxi, r.from_dxi[l], dxi.astype(f32), 0)
        back = back + matmul(dxi, r.w_x[l], COLS_COLS)

        if l == last:
            drive(normed_tasks[last])
            gated_copies[0].wait_recv()
            gated_copies[last].wait_recv()
            statistic.wait_recv()
            stat = column(r.statin[last][z.tensor_bits][...])
            their_f = lax.rsqrt(stat[:, 0:1] / inner + EPSILON)
            wout_product(l, db, (r.from_db[l][...] * their_f).astype(bf16))
        else:
            step(db_task)

        dlog = exact(dys.astype(f32) * within - xdt.astype(f32) * dxdt, spread)
        drate = exact(lower, dlog, ROWS_ROWS)
        ddt = exact(dxdt * xc, spread) + drate * neg
        draw = ddt * sigmoid(raw)
        ddti = draw.astype(bf16)
        back = back + matmul(ddti, r.wdt[l])

        dscores = dscores.astype(SCAN)
        dkeys = scan_dot(dscores, queries, ROWS_ROWS)
        dqueries = scan_dot(dscores, keys)
        dbcc = jnp.concatenate([dkeys, dqueries], axis=1)
        dpre_b = dbcc * (sb * (1.0 + pre_b * (1.0 - sb)))
        dbci = conv_back(taps_b, dpre_b).astype(bf16)
        k = 2 * LAYERS - 1 - l
        back = back + matmul(dbci, r.w_bc[l], COLS_COLS)
        back_task = flow.row_sum(k, back, full[k])
        step(back_task)
        if l == last:
            step(output_task)
        step(back_task)
        for t in range(z.tensor):
            picked = matmul(normed, pick_shared(t)).astype(bf16)
            group = z.dp * z.cutp
            r.sum_wbc[l][t * group : (t + 1) * group, :] = matmul(picked, dbci, ROWS_ROWS)

        bits = flow.every(TENSOR) + flow.every(DP)
        tasks["b", l] = flow.scatter(
            r.sum_wbc[l], r.in_wbc[l], bits, finish_to("b", l, z.cut)
        )
        step(tasks["b", l])
        sides = (
            (slice(0, channels), r.xi[l], dpre_x),
            (slice(width - both, width), r.bci[l], dpre_b),
        )
        for at, signal, back_pre in sides:
            for tap in range(K):
                small[tap : tap + 1, at] = jnp.sum(
                    back_pre * delayed(signal, K - 1 - tap), axis=0, keepdims=True
                )
            small[K : K + 1, at] = jnp.sum(back_pre, axis=0, keepdims=True)
        small[K + 1 : K + 2, :channels] = jnp.sum(dgated * core, axis=0, keepdims=True)
        at = slice(channels, channels + LANES)
        small[0:1, at] = jnp.sum(drate * rate, axis=0, keepdims=True)
        small[1:2, at] = exact(jnp.sum(dy * xc, axis=0, keepdims=True) + jnp.zeros((8, 1), f32), spread)[0:1, :]
        small[2:3, at] = jnp.sum(draw, axis=0, keepdims=True)
        small[8:, :] = matmul(ddti, normed, ROWS_ROWS)[: z.head_rows, :]
        if l == last:
            weight_product("z", l, copies["z", l])
            drive(output_task)
            for i in range(CHUNKS):
                flow.release((id(r.output), i))
            r.output[...] = residual(l) + f * r.output[...]
        else:
            step(tasks["o", last])
            step(tasks["z", last])
            drive(db_task)
            wout_product(l, db, r.from_db[l][...].astype(bf16))
            weight_product("z", l, copies["z", l])
            step(tasks["b", last])
            step(tasks["s", last])
            step(tasks["x", last])
            step(tasks["o", last])
        step(tasks["b", l])
        drive(back_task)

        h = residual(l)
        back_normed = full[k][...]
        scale = lax.rsqrt(jnp.mean(h * h, axis=1, keepdims=True) + EPSILON)
        small[6:7, :] = jnp.sum(back_normed * h * scale, axis=0, keepdims=True)
        tasks["s", l] = small_task(l)
        step(tasks["s", l])
        hat = back_normed * r.norm_gain[l : l + 1, :]
        return g + scale * hat - scale * scale * scale * h * jnp.mean(
            hat * h, axis=1, keepdims=True
        )

    g = r.cotangent[...].astype(f32)
    for l in reversed(range(LAYERS)):
        g = backward(l, g)
    for i in range(CHUNKS):
        flow.release((id(r.input_grad), i))
    r.input_grad[...] = g
    weight_product("x", 0, copies["x", 0])
    pending = [tasks[m, l] for m, l in TAIL]
    while pending:
        left = []
        for task in pending:
            if next(task, pending) is not pending:
                left.append(task)
        pending = left
    flow.drain()


TAIL = (("z", 0), ("s", 0), ("x", 0), ("o", 0), ("b", 0)) + tuple((m, LAYERS - 1) for m in "xzosb")


def deliver_kernel(count, *refs):
    for i in range(count):
        refs[count + i][...] = refs[i][...]


def on_device(dp_size, tensor_size, *args):
    given = Inputs(*args)
    rows, width = given.tokens.shape
    z = Sizes(
        dp_size,
        tensor_size,
        rows,
        width,
        given.w_z.shape[2],
        given.w_bc.shape[2],
        given.w_dt.shape[2],
    )
    given = given._replace(w_dt=jnp.transpose(given.w_dt, (2, 0, 1)))
    outs = out_shapes(z)
    results = pl.pallas_call(
        functools.partial(fused_kernel, z),
        out_shape=outs,
        in_specs=[pl.BlockSpec(memory_space=pltpu.VMEM)] * len(args),
        out_specs=[pl.BlockSpec(memory_space=pltpu.VMEM)] * len(outs),
        scratch_shapes=list(scratch_shapes(z)),
        compiler_params=pltpu.CompilerParams(
            collective_id=0, has_side_effects=True, vmem_limit_bytes=63 * 1024 * 1024
        ),
    )(*given)
    results = pl.pallas_call(
        functools.partial(deliver_kernel, len(outs)),
        out_shape=outs,
        in_specs=[pl.BlockSpec(memory_space=pltpu.VMEM)] * len(outs),
        out_specs=[pl.BlockSpec(memory_space=pltpu.VMEM)] * len(outs),
    )(*results)
    done = Outputs(*results)
    return tuple(
        done._replace(
            g_wdt=jnp.transpose(done.g_wdt, (1, 2, 0)),
            g_wout=jnp.swapaxes(done.g_wout, 1, 2),
            g_chan=jnp.transpose(done.g_chan, (2, 0, 1, 3)),
            g_bcc=jnp.swapaxes(done.g_bcc, 0, 1),
            g_heads=jnp.swapaxes(done.g_heads, 0, 1),
        )
    )


def solution(mesh):
    placed = (
        P(DP, None),
        P(DP, None),
        P(),
        P(None, None, TENSOR),
        P(None, None, TENSOR),
        P(),
        P(None, None, TENSOR),
        P(None, None, TENSOR),
        P(None, TENSOR),
        P(),
        P(),
        P(None, TENSOR),
        P(None, TENSOR),
        P(None, TENSOR),
        P(None, TENSOR),
        P(None, TENSOR, None),
    )
    return jax.shard_map(
        functools.partial(on_device, mesh.shape[DP], mesh.shape[TENSOR]),
        mesh=mesh,
        in_specs=placed,
        out_specs=(
            P(DP, None),
            P(DP, None),
            P(None, DP),
            P(None, DP, TENSOR),
            P(None, DP, TENSOR),
            P(None, DP, TENSOR),
            P(None, TENSOR, DP),
            P(None, None, TENSOR, DP),
            P(None, (DP, TENSOR), None),
            P(None, None, (DP, TENSOR)),
            P(None, None, TENSOR),
        ),
        check_vma=False,
    )
```
